512 devices in a mesh: tile: 128 (over z, x, core), lev: 4 (over y).
Axes of the slice: x: 4, y: 4, z: 16, core: 2. Of those that a mesh axis runs over, the one named last changes fastest.
Arguments:
- probes: bfloat16 [512, 32, 8, 128], P('tile', None, 'lev'), may hold values from -1 to 1, as said below
- stddev: float32 [512, 32, 128], P('tile'), may hold values from 0.5 to 2
- diffusivity: float32 [128], replicated, may hold values from 0.03 to 0.24
- counts: int32 [128, 128], P('tile'), may hold values from 0 to 16, as said below
- columns: int32 [128, 128, 16], P('tile'), may hold values from 0 to 127
- jacobian: bfloat16 [128, 256, 32], P('tile'), may hold values from -1 to 1
- offsets: int32 [128, 256], replicated, may hold values from 0 to 96
- obs_weights: float32 [128, 256], replicated, may hold values from 0.25 to 4
Outputs:
- hessian_probe: float32 [512, 32, 8, 128], P('tile', None, 'lev')
- trace_share: float32 [128], P('tile')
The draws below stay inside these ranges and needn't reach their ends.
Inputs may be any that keep to these rules, and one draw needn't show every extreme that they name: `counts`: in every draw one section receives 16 observations from every tile. `columns`: slots at or past counts[t,d] are unused. `probes`: each entry is +1 or -1.
All inputs are finite; a program needn't handle non-finite values.
Results may differ from the reference program's by a relative error of at most 0.00045.
The reference program's roundings to bfloat16 on the way count: a program that leaves them out, or rounds other values in their place, can miss the bound.
Values may be sent and summed in bfloat16 or wider, within the bound.
No kernel may reach another device: no remote copies, remote signals or barrier semaphores. Data moves between devices by JAX's collectives and lax.ppermute only.
A program may use at most 64 MiB of HBM per device.

```python
import math
import jax
import jax.numpy as jnp
from jax import lax

CX = 4
CY = 32
CAP = 16
LEV = 128
CH = 256
BAND = 32
PROBES = 8
NSTEP = 2
TILES = 128
NX = 512
N_TILE = 128


def draw_counts(key, part):
    key_load = jax.random.fold_in(key, 11)
    key_fill = jax.random.fold_in(key, 12)
    key_full = jax.random.fold_in(key, 13)
    loading = jax.random.randint(key_load, (TILES,), 1, 5)
    lowest = CAP * loading // 8
    highest = CAP * loading // 4 + 1
    raw_bits = jax.random.randint(key_fill, (TILES, TILES), 0, 1 << 30)
    filled = lowest[None, :] + raw_bits % (highest - lowest)[None, :]
    busiest = jax.random.randint(key_full, (), 0, TILES)
    sections = jnp.arange(TILES)
    filled = jnp.where(sections[None, :] == busiest, CAP, filled)
    return filled.astype(jnp.int32)


def draw_probes(key, part):
    coin_flips = jax.random.randint(key, (NX, CY, PROBES, LEV), 0, 2)
    return (2.0 * coin_flips.astype(jnp.float32) - 1.0).astype(jnp.bfloat16)


def place_ends(entries, rng, low, largest):
    longest = entries.shape.index(max(entries.shape))
    spots = []
    for shift in (0, 1):
        where = [jax.random.randint(jax.random.fold_in(rng, axis), (), 0, length) for axis, length in enumerate(entries.shape)]
        where[longest] = (where[longest] + shift) % entries.shape[longest]
        spots.append(tuple(where))
    return entries.at[spots[0]].set(low).at[spots[1]].set(largest)


def block_levels(own_key, extent, shards, smallest, top_value):
    gain = 1.0
    for position, parts in shards:
        steps = jax.random.uniform(jax.random.fold_in(jax.random.fold_in(own_key, 6), position), (parts,), jnp.float32, smallest / len(shards), top_value / len(shards))
        gain = gain * jnp.repeat(jnp.exp(steps), extent[position] // parts).reshape((-1,) + (1,) * (len(extent) - 1 - position))
    return gain


def gaussian(own_key, extent, deviation, reach, split=(), kind=jnp.bfloat16):
    entries = jax.random.normal(own_key, extent, jnp.float32) * deviation
    if len(split) > 0:
        entries = block_levels(own_key, extent, split, -0.22, 0.18) * entries
    return jnp.clip(entries, min=-reach, max=reach).astype(kind)


def setup_inputs(seed: int = 0) -> dict:
    key_list = jax.random.split(jax.random.key(seed), 9)
    return {
        "probes": draw_probes(jax.random.fold_in(key_list[8], 71), 0),
        "stddev": jnp.clip(jnp.exp(math.log(2.0) - 1.3862944 * jax.random.uniform(key_list[1], (NX, CY, LEV), jnp.float32) ** block_levels(key_list[1], (NX, CY, LEV), ((0, 128),), -0.2, 0.2)), 0.5, 2.0),
        "diffusivity": jnp.clip(jnp.exp(jax.random.uniform(key_list[2], (LEV,), jnp.float32, math.log(0.03), math.log(0.24))), 0.03, 0.24),
        "counts": draw_counts(jax.random.fold_in(key_list[8], 71), 0),
        "columns": place_ends(jax.random.randint(key_list[4], (TILES, TILES, CAP), 0, CX * CY), jax.random.fold_in(key_list[4], 1), 0, (CX * CY) - 1).astype(jnp.int32),
        "jacobian": gaussian(key_list[5], (TILES, CH, BAND), BAND ** -0.5, 1.0, ((0, 128),)),
        "offsets": place_ends(jax.random.randint(key_list[6], (TILES, CH), 0, LEV - BAND + 1), jax.random.fold_in(key_list[6], 1), 0, LEV - BAND).astype(jnp.int32),
        "obs_weights": jnp.clip(jnp.exp(jax.random.uniform(key_list[7], (TILES, CH), jnp.float32, math.log(0.25), math.log(4.0))), 0.25, 4.0),
    }


def diffuse(extended, diffusivity):
    middle = extended[1:-1]
    padded = jnp.pad(middle, ((0, 0), (1, 1), (0, 0), (0, 0)))
    laplace = extended[2:] + extended[:-2] + padded[:, 2:] + padded[:, :-2] - 4.0 * middle
    return middle + diffusivity * laplace


def smooth(profile, diffusivity):
    for repeat in range(NSTEP):
        extended = jnp.concatenate([profile[-1:], profile, profile[:1]], axis=0)
        profile = diffuse(extended, diffusivity)
    return profile


def band_matrix(jacobian_rows, offset_rows):
    band_width = jacobian_rows.shape[-1]
    shifted = jnp.arange(LEV, dtype=jnp.int32) - offset_rows[..., None]
    inside = (shifted >= 0) & (shifted < band_width)
    picked = jnp.take_along_axis(jacobian_rows, jnp.clip(shifted, 0, band_width - 1).astype(jnp.int32), axis=-1)
    return jnp.where(inside, picked, jnp.zeros_like(picked))


def respond(rows_in, dense_map, weights):
    brightness = jnp.dot(rows_in, dense_map.T, preferred_element_type=jnp.float32)
    weighted = weights * brightness
    energy = jnp.sum(brightness * weighted, axis=1)
    adjoint = jnp.dot(weighted.astype(jnp.bfloat16), dense_map, preferred_element_type=jnp.float32)
    return adjoint.astype(jnp.bfloat16), energy


def reference(probes, stddev, diffusivity, counts, columns, jacobian, offsets, obs_weights):
    spread = stddev[:, :, None, :]
    profile = (spread * smooth(probes.astype(jnp.float32), diffusivity)).astype(jnp.bfloat16)
    tiles_view = profile.reshape(N_TILE, CX * CY, PROBES, LEV)
    slot_ids = jnp.arange(CAP, dtype=jnp.int32)
    tile_ids = jnp.arange(N_TILE, dtype=jnp.int32)

    def section(carry_sum, section_id):
        cols_here = columns[:, section_id, :]
        live_slots = slot_ids[None, :] < counts[:, section_id][:, None]
        rows_here = tiles_view[tile_ids[:, None], cols_here]
        rows_here = jnp.where(live_slots[:, :, None, None], rows_here, jnp.zeros_like(rows_here))
        dense_map = band_matrix(jacobian[section_id], offsets[section_id])
        adjoint, energy = respond(rows_here.reshape(-1, LEV), dense_map, obs_weights[section_id])
        adjoint = adjoint.reshape(N_TILE, CAP, PROBES, LEV).astype(jnp.float32)
        carry_sum = carry_sum.at[tile_ids[:, None], cols_here].add(adjoint)
        return carry_sum, jnp.sum(energy)

    start_sum = jnp.zeros((N_TILE, CX * CY, PROBES, LEV), jnp.float32)
    summed, energies = lax.scan(section, start_sum, tile_ids)
    gradient = summed.reshape(NX, CY, PROBES, LEV)
    hessian = smooth(spread * gradient, diffusivity)
    trace_share = energies * (1.0 / (PROBES * N_TILE * CAP * CH))
    return hessian, trace_share
```

```python
import jax
import jax.numpy as jnp
from jax import lax
from jax.experimental import pallas as pl
from jax.experimental.pallas import tpu as pltpu
from jax.sharding import PartitionSpec as P

NSTEP = 2
ZS, XS, CS = 16, 4, 2
QS = XS * CS


def tile_groups(sizes, free):
    groups = {}
    for z in range(sizes[0]):
        for x in range(sizes[1]):
            for c in range(sizes[2]):
                key = tuple(v for i, v in enumerate((z, x, c)) if i not in free)
                groups.setdefault(key, []).append((z * sizes[1] + x) * sizes[2] + c)
    return list(groups.values())


def laplace_step(ext, diffusivity):
    middle = ext[:, 1:-1]
    padded = jnp.pad(middle, ((0, 0), (0, 0), (1, 1), (0, 0)))
    laplace = ext[:, 2:] + ext[:, :-2] + padded[:, :, 2:] + padded[:, :, :-2] - 4.0 * middle
    return middle + diffusivity * laplace


def halo(field, width):
    count = lax.axis_size("tile")
    before = lax.ppermute(field[:, -width:], "tile", [(i, (i + 1) % count) for i in range(count)])
    after = lax.ppermute(field[:, :width], "tile", [((i + 1) % count, i) for i in range(count)])
    return before, after


def smooth(field, diffusivity):
    before, after = halo(field, NSTEP)
    ext = jnp.concatenate([before, field, after], axis=1).astype(jnp.float32)
    for _ in range(NSTEP):
        ext = laplace_step(ext, diffusivity)
    return ext


def band_columns(jac, offsets):
    band, ch = jac.shape

    def zeros(n):
        return jnp.zeros((n, ch), jac.dtype)

    x = jnp.concatenate([jac, zeros(8)], axis=0)
    for shift in (1, 2, 4):
        x = jnp.where((offsets & shift) != 0, pltpu.roll(x, shift, 0), x)
    for shift in (8, 16, 32):
        down = jnp.concatenate([zeros(shift), x], axis=0)
        stay = jnp.concatenate([x, zeros(shift)], axis=0)
        x = jnp.where((offsets & shift) != 0, down, stay)
    far = (offsets & 64) != 0
    top = jnp.where(far, zeros(64), x[:64])
    low = jnp.where(far, x[:64], jnp.concatenate([x[64:96], zeros(32)], axis=0))
    return jnp.concatenate([top, low], axis=0)


def respond_kernel(me_ref, gathered, jac, off, wts, mine, other, energy, sel, rows, adj):
    tiles, cells_ext, width = gathered.shape
    cells = sel.shape[1]
    sections = jac.shape[0]
    lev = width // 2
    slot = rows.shape[1] // sections
    me = me_ref[0]
    cell_id = lax.broadcasted_iota(jnp.int32, (cells, rows.shape[1]), 0).astype(jnp.float32)
    pick = lax.broadcasted_iota(jnp.int32, (tiles, width), 0) == me
    for q in range(tiles):
        block = gathered[q, cells : cells + tiles, :].astype(jnp.float32)
        target = jnp.sum(jnp.where(pick, block, 0.0), axis=0, keepdims=True)
        chosen = jnp.where(cell_id == target, 1.0, 0.0).astype(jnp.bfloat16)
        sel[q] = chosen
        rows[q] = lax.dot_general(
            chosen,
            gathered[q, :cells, :],
            (((0,), (0,)), ((), ())),
            preferred_element_type=jnp.float32,
        ).astype(jnp.bfloat16)
    for s in range(sections):
        band = band_columns(jac[s].astype(jnp.float32), off[s : s + 1, :]).astype(jnp.bfloat16)
        here = slice(s * slot, (s + 1) * slot)
        weight = wts[s : s + 1, :]
        total = jnp.zeros((1, band.shape[1]), jnp.float32)
        for h in range(2):
            span = range(h * tiles // 2, (h + 1) * tiles // 2)
            mine_rows = jnp.concatenate(
                [rows[q, here, p * lev : (p + 1) * lev] for q in span for p in range(2)], axis=0
            )
            bright = jnp.dot(mine_rows, band, preferred_element_type=jnp.float32)
            weighted = weight * bright
            total = total + jnp.sum(bright * weighted, axis=0, keepdims=True)
            back = lax.dot_general(
                weighted.astype(jnp.bfloat16),
                band,
                (((1,), (1,)), ((), ())),
                preferred_element_type=jnp.float32,
            ).astype(jnp.bfloat16)
            at = 0
            for q in span:
                for p in range(2):
                    adj[q, here, p * lev : (p + 1) * lev] = back[at : at + slot]
                    at += slot
        energy[s : s + 1, :] = total
    for j in range(tiles // 2):
        for half, out in ((0, mine), (1, other)):
            q = 2 * j + jnp.where(half == 0, me % 2, 1 - me % 2)
            out[j] = jnp.dot(sel[q], adj[q], preferred_element_type=jnp.float32)


def respond_all(me, gathered, jac, off, wts):
    tiles, cells_ext, width = gathered.shape
    cells = cells_ext - tiles
    sections = jac.shape[0]
    part = jax.ShapeDtypeStruct((tiles // 2, cells, width), jnp.float32)
    vmem = pl.BlockSpec(memory_space=pltpu.VMEM)
    return pl.pallas_call(
        respond_kernel,
        out_shape=(part, part, jax.ShapeDtypeStruct((sections, wts.shape[1]), jnp.float32)),
        in_specs=[pl.BlockSpec(memory_space=pltpu.SMEM), vmem, vmem, vmem, vmem],
        out_specs=(vmem, vmem, vmem),
        scratch_shapes=[
            pltpu.VMEM((tiles, cells, 256), jnp.bfloat16),
            pltpu.VMEM((tiles, 256, width), jnp.bfloat16),
            pltpu.VMEM((tiles, 256, width), jnp.bfloat16),
        ],
        name="respond",
    )(me, gathered, jac, off, wts)


def body(probes, stddev, diffusivity, counts, columns, jacobian, offsets, obs_weights):
    tile_count = lax.axis_size("tile")
    row_count, col_count, probe_count, levels = probes.shape
    slot_count = columns.shape[2]
    channels = jacobian.shape[1]
    cell_count = row_count * col_count
    sizes = (ZS, XS, CS)
    along_z = tile_groups(sizes, (0,))
    along_x = tile_groups(sizes, (1,))
    plane = tile_groups(sizes, (1, 2))
    here = lax.axis_index("tile")
    me = here % QS
    own = jnp.swapaxes(jacobian, 1, 2)
    jac = lax.all_to_all(
        jnp.broadcast_to(own, (ZS,) + own.shape[1:]),
        "tile", 0, 0, axis_index_groups=along_z, tiled=True,
    )
    live = jnp.arange(slot_count, dtype=jnp.int32)[None, :] < counts[0][:, None]
    target = jnp.where(live, columns[0], -1).astype(jnp.bfloat16)
    target = target.reshape(ZS, QS, slot_count).swapaxes(0, 1).reshape(QS, ZS * slot_count)
    field = probes.transpose(2, 0, 1, 3)
    profile = (stddev[None] * smooth(field, diffusivity)).astype(jnp.bfloat16)
    profile = profile.transpose(1, 2, 0, 3).reshape(cell_count, probe_count * levels)
    gathered = lax.all_gather(
        jnp.concatenate([profile, target], axis=0)[None],
        "tile", axis=0, axis_index_groups=plane, tiled=True,
    )
    off = lax.dynamic_index_in_dim(offsets.reshape(ZS, QS, channels), me, 1, keepdims=False)
    wts = lax.dynamic_index_in_dim(obs_weights.reshape(ZS, QS, channels), me, 1, keepdims=False)
    mine, other, energy = respond_all(me.reshape(1), gathered, jac, off, wts)
    lev_count = lax.axis_size("lev")
    along_zy = [[t * lev_count + y for t in group for y in range(lev_count)] for group in along_z]
    spread = jnp.repeat(jnp.sum(energy, axis=1), lev_count)
    shares = lax.all_to_all(spread, ("tile", "lev"), 0, 0, axis_index_groups=along_zy, tiled=True)
    trace_share = (
        jnp.sum(shares) * (1.0 / (probe_count * lev_count * tile_count * slot_count * channels))
    ).reshape(1)
    summed = mine + lax.ppermute(other, "tile", [(i, i ^ 1) for i in range(tile_count)])
    parts = lax.all_to_all(summed, "tile", 0, 0, axis_index_groups=along_x, tiled=True)
    gradient = jnp.sum(parts, axis=0).reshape(row_count, col_count, probe_count, levels)
    hessian = smooth(stddev[None] * gradient.transpose(2, 0, 1, 3), diffusivity)
    return (hessian.transpose(1, 2, 0, 3), trace_share)


def solution(mesh):
    placed = (
        P("tile", None, "lev", None),
        P("tile", None, None),
        P(),
        P("tile", None),
        P("tile", None, None),
        P("tile", None, None),
        P(),
        P(),
    )
    return jax.shard_map(
        body,
        mesh=mesh,
        in_specs=placed,
        out_specs=(P("tile", None, "lev", None), P("tile")),
        check_vma=False,
    )
```

```python
import jax
import jax.numpy as jnp
from jax import lax
from jax.experimental import pallas as pl
from jax.experimental.pallas import tpu as pltpu
from jax.sharding import PartitionSpec as P

NSTEP = 2
ZS, XS, CS = 16, 4, 2
QS = XS * CS


def tile_groups(sizes, free):
    groups = {}
    for z in range(sizes[0]):
        for x in range(sizes[1]):
            for c in range(sizes[2]):
                key = tuple(v for i, v in enumerate((z, x, c)) if i not in free)
                groups.setdefault(key, []).append((z * sizes[1] + x) * sizes[2] + c)
    return list(groups.values())


def laplace_step(ext, diffusivity):
    middle = ext[:, 1:-1]
    padded = jnp.pad(middle, ((0, 0), (0, 0), (1, 1), (0, 0)))
    laplace = ext[:, 2:] + ext[:, :-2] + padded[:, :, 2:] + padded[:, :, :-2] - 4.0 * middle
    return middle + diffusivity * laplace


def halo(field, width):
    count = lax.axis_size("tile")
    even = (lax.axis_index("tile") & 1) == 0
    top, bottom = field[:, :width], field[:, -width:]
    cross = lax.ppermute(
        jnp.where(even, top, bottom),
        "tile",
        [(i, (i - 1 if i % 2 == 0 else i + 1) % count) for i in range(count)],
    )
    near = lax.ppermute(jnp.where(even, bottom, top), "tile", [(i, i ^ 1) for i in range(count)])
    return jnp.where(even, cross, near), jnp.where(even, near, cross)


def smooth(field, diffusivity):
    before, after = halo(field, NSTEP)
    ext = jnp.concatenate([before, field, after], axis=1).astype(jnp.float32)
    for _ in range(NSTEP):
        ext = laplace_step(ext, diffusivity)
    return ext


def band_columns(jac, offsets):
    band, ch = jac.shape

    def zeros(n):
        return jnp.zeros((n, ch), jac.dtype)

    x = jnp.concatenate([jac, zeros(8)], axis=0)
    for shift in (1, 2, 4):
        x = jnp.where((offsets & shift) != 0, pltpu.roll(x, shift, 0), x)
    for shift in (8, 16, 32):
        down = jnp.concatenate([zeros(shift), x], axis=0)
        stay = jnp.concatenate([x, zeros(shift)], axis=0)
        x = jnp.where((offsets & shift) != 0, down, stay)
    far = (offsets & 64) != 0
    top = jnp.where(far, zeros(64), x[:64])
    low = jnp.where(far, x[:64], jnp.concatenate([x[64:96], zeros(32)], axis=0))
    return jnp.concatenate([top, low], axis=0)


def respond_kernel(me_ref, gathered, jac, off, wts, mine, other, energy, sel, rows, adj):
    tiles, cells_ext, width = gathered.shape
    cells = sel.shape[1]
    sections = jac.shape[0]
    lev = width // 2
    slot = rows.shape[1] // sections
    me = me_ref[0]
    cell_id = lax.broadcasted_iota(jnp.int32, (cells, rows.shape[1]), 0).astype(jnp.float32)
    pick = lax.broadcasted_iota(jnp.int32, (tiles, width), 0) == me
    for q in range(tiles):
        block = gathered[q, cells : cells + tiles, :].astype(jnp.float32)
        target = jnp.sum(jnp.where(pick, block, 0.0), axis=0, keepdims=True)
        chosen = jnp.where(cell_id == target, 1.0, 0.0).astype(jnp.bfloat16)
        sel[q] = chosen
        rows[q] = lax.dot_general(
            chosen,
            gathered[q, :cells, :],
            (((0,), (0,)), ((), ())),
            preferred_element_type=jnp.float32,
        ).astype(jnp.bfloat16)
    for s in range(sections):
        row = pl.ds(s * tiles + me, 1)
        band = band_columns(jac[s].astype(jnp.float32), off[row, :]).astype(jnp.bfloat16)
        here = slice(s * slot, (s + 1) * slot)
        weight = wts[row, :]
        total = jnp.zeros((1, band.shape[1]), jnp.float32)
        for h in range(2):
            span = range(h * tiles // 2, (h + 1) * tiles // 2)
            mine_rows = jnp.concatenate(
                [rows[q, here, p * lev : (p + 1) * lev] for q in span for p in range(2)], axis=0
            )
            bright = jnp.dot(mine_rows, band, preferred_element_type=jnp.float32)
            weighted = weight * bright
            total = total + jnp.sum(bright * weighted, axis=0, keepdims=True)
            back = lax.dot_general(
                weighted.astype(jnp.bfloat16),
                band,
                (((1,), (1,)), ((), ())),
                preferred_element_type=jnp.float32,
            ).astype(jnp.bfloat16)
            at = 0
            for q in span:
                for p in range(2):
                    adj[q, here, p * lev : (p + 1) * lev] = back[at : at + slot]
                    at += slot
        each = energy.shape[0] // sections
        energy[s * each : (s + 1) * each] = jnp.broadcast_to(
            jnp.sum(total, axis=1, keepdims=True)[None], (each,) + energy.shape[1:]
        )
    for j in range(tiles // 2):
        for half, out in ((0, mine), (1, other)):
            q = 2 * j + ((me & 1) if half == 0 else 1 - (me & 1))
            out[j] = jnp.dot(sel[q], adj[q], preferred_element_type=jnp.float32)


def respond_all(me, gathered, jac, off, wts, copies):
    tiles, cells_ext, width = gathered.shape
    cells = cells_ext - tiles
    sections = jac.shape[0]
    part = jax.ShapeDtypeStruct((tiles // 2, cells, width), jnp.float32)
    vmem = pl.BlockSpec(memory_space=pltpu.VMEM)
    return pl.pallas_call(
        respond_kernel,
        out_shape=(part, part, jax.ShapeDtypeStruct((sections * copies, 8, 128), jnp.float32)),
        in_specs=[pl.BlockSpec(memory_space=pltpu.SMEM), vmem, vmem, vmem, vmem],
        out_specs=(vmem, vmem, vmem),
        scratch_shapes=[
            pltpu.VMEM((tiles, cells, 256), jnp.bfloat16),
            pltpu.VMEM((tiles, 256, width), jnp.bfloat16),
            pltpu.VMEM((tiles, 256, width), jnp.bfloat16),
        ],
        name="respond",
    )(me, gathered, jac, off, wts)


def body(probes, stddev, diffusivity, counts, columns, jacobian, offsets, obs_weights):
    tile_count = lax.axis_size("tile")
    row_count, col_count, probe_count, levels = probes.shape
    slot_count = columns.shape[2]
    channels = jacobian.shape[1]
    cell_count = row_count * col_count
    sizes = (ZS, XS, CS)
    along_z = tile_groups(sizes, (0,))
    along_x = tile_groups(sizes, (1,))
    plane = tile_groups(sizes, (1, 2))
    here = lax.axis_index("tile")
    me = here & (QS - 1)
    own = jnp.swapaxes(jacobian, 1, 2)
    jac = lax.all_to_all(
        jnp.broadcast_to(own, (ZS,) + own.shape[1:]),
        "tile", 0, 0, axis_index_groups=along_z, tiled=True,
    )
    live = jnp.arange(slot_count, dtype=jnp.int32)[None, :] < counts[0][:, None]
    target = jnp.where(live, columns[0], -1).astype(jnp.bfloat16)
    target = target.reshape(ZS, QS, slot_count).swapaxes(0, 1).reshape(QS, ZS * slot_count)
    field = probes.transpose(2, 0, 1, 3)
    profile = (stddev[None] * smooth(field, diffusivity)).astype(jnp.bfloat16)
    profile = profile.transpose(1, 2, 0, 3).reshape(cell_count, probe_count * levels)
    gathered = lax.all_gather(
        jnp.concatenate([profile, target], axis=0)[None],
        "tile", axis=0, axis_index_groups=plane, tiled=True,
    )
    lev_count = lax.axis_size("lev")
    mine, other, energy = respond_all(me.reshape(1), gathered, jac, offsets, obs_weights, lev_count)
    along_zy = [[t * lev_count + y for t in group for y in range(lev_count)] for group in along_z]
    shares = lax.all_to_all(energy, ("tile", "lev"), 0, 0, axis_index_groups=along_zy, tiled=True)
    trace_share = (
        jnp.sum(shares[:, 0, 0])
        * (1.0 / (probe_count * lev_count * tile_count * slot_count * channels))
    ).reshape(1)
    summed = mine + lax.ppermute(other, "tile", [(i, i ^ 1) for i in range(tile_count)])
    x = (here >> 1) & (XS - 1)
    gradient = lax.dynamic_index_in_dim(summed, x, 0, keepdims=False)
    for step in range(1, XS):
        ring = [(i, i // QS * QS + (i + step * CS) % QS) for i in range(tile_count)]
        sent = lax.dynamic_index_in_dim(summed, (x + step) & (XS - 1), 0, keepdims=False)
        gradient = gradient + lax.ppermute(sent, "tile", ring)
    gradient = gradient.reshape(row_count, col_count, probe_count, levels)
    hessian = smooth(stddev[None] * gradient.transpose(2, 0, 1, 3), diffusivity)
    return (hessian.transpose(1, 2, 0, 3), trace_share)


def solution(mesh):
    placed = (
        P("tile", None, "lev", None),
        P("tile", None, None),
        P(),
        P("tile", None),
        P("tile", None, None),
        P("tile", None, None),
        P(),
        P(),
    )
    return jax.shard_map(
        body,
        mesh=mesh,
        in_specs=placed,
        out_specs=(P("tile", None, "lev", None), P("tile")),
        check_vma=False,
    )
```

```python
import jax
import jax.numpy as jnp
from jax import lax
from jax.experimental import pallas as pl
from jax.experimental.pallas import tpu as pltpu
from jax.sharding import PartitionSpec as P

NSTEP = 2
ZS, XS, CS = 16, 4, 2
QS = XS * CS


def tile_groups(sizes, free):
    groups = {}
    for z in range(sizes[0]):
        for x in range(sizes[1]):
            for c in range(sizes[2]):
                key = tuple(v for i, v in enumerate((z, x, c)) if i not in free)
                groups.setdefault(key, []).append((z * sizes[1] + x) * sizes[2] + c)
    return list(groups.values())


def laplace_step(ext, diffusivity):
    middle = ext[1:-1]
    padded = jnp.pad(middle, ((0, 0), (1, 1), (0, 0), (0, 0)))
    laplace = ext[2:] + ext[:-2] + padded[:, 2:] + padded[:, :-2] - 4.0 * middle
    return middle + diffusivity * laplace


def edge_rows(field, width):
    even = (lax.axis_index("tile") & 1) == 0
    top, bottom = field[:width], field[-width:]
    return jnp.where(even, top, bottom), jnp.where(even, bottom, top)


def swap_edges(to_cross, to_near):
    count = lax.axis_size("tile")
    across = [(i, (i - 1 if i % 2 == 0 else i + 1) % count) for i in range(count)]
    cross = lax.ppermute(to_cross, "tile", across)
    near = lax.ppermute(to_near, "tile", [(i, i ^ 1) for i in range(count)])
    return cross, near


def smooth(field, diffusivity):
    cross, near = swap_edges(*edge_rows(field, NSTEP))
    even = (lax.axis_index("tile") & 1) == 0
    ext = jnp.concatenate(
        [jnp.where(even, cross, near), field, jnp.where(even, near, cross)], axis=0
    )
    for _ in range(NSTEP):
        ext = laplace_step(ext, diffusivity)
    return ext


def profile_kernel(me_ref, field, cross, near, stddev, diffusivity, columns, counts, out):
    tile_rows, cols, lev = stddev.shape
    wide = 2 * cols
    edge = cross.shape[0]
    even = (me_ref[0] & 1) == 0
    before = jnp.where(even, cross[...], near[...])
    after = jnp.where(even, near[...], cross[...])
    own = field[...]
    left = lax.broadcasted_iota(jnp.int32, (wide, wide), 0)
    right = lax.broadcasted_iota(jnp.int32, (wide, wide), 1)
    split = jnp.where(
        right == jnp.where(left < cols, 2 * left, 2 * (left - cols) + 1), 1.0, 0.0
    ).astype(jnp.bfloat16)
    grid = []
    for block, count in ((before, edge // wide), (own, tile_rows), (after, edge // wide)):
        for i in range(count):
            grid.append(
                jnp.dot(split, block[i * wide : (i + 1) * wide], preferred_element_type=jnp.float32)
            )
    place = lax.broadcasted_iota(jnp.int32, (wide, lev), 0) & (cols - 1)
    rate = diffusivity[...]
    for _ in range(NSTEP):
        new = []
        for i in range(1, len(grid) - 1):
            middle = grid[i]
            following = jnp.where(place == cols - 1, 0.0, pltpu.roll(middle, wide - 1, 0))
            leading = jnp.where(place == 0, 0.0, pltpu.roll(middle, 1, 0))
            laplace = grid[i + 1] + grid[i - 1] + following + leading - 4.0 * middle
            new.append(middle + rate * laplace)
        grid = new
    for i in range(tile_rows):
        for p in range(2):
            out[i * cols : (i + 1) * cols, p * lev : (p + 1) * lev] = (
                stddev[i] * grid[i][p * cols : (p + 1) * cols]
            ).astype(jnp.bfloat16)
    slots, sections = columns.shape
    width = out.shape[1]
    live = lax.broadcasted_iota(jnp.int32, (slots, sections), 0) < counts[...]
    target = jnp.where(live, columns[...], -1).astype(jnp.float32).astype(jnp.bfloat16)
    lane = lax.broadcasted_iota(jnp.int32, (sections, width), 1)
    apart = lax.broadcasted_iota(jnp.int32, (sections, width), 0) - (lane >> 4) * QS
    slot = lax.broadcasted_iota(jnp.int32, (slots, width), 0)
    mine = slot == (lax.broadcasted_iota(jnp.int32, (slots, width), 1) & (slots - 1))
    lines = []
    for q in range(QS):
        choose = jnp.where(apart == q, 1.0, 0.0).astype(jnp.bfloat16)
        spread = jnp.dot(target, choose, preferred_element_type=jnp.float32)
        lines.append(jnp.sum(jnp.where(mine, spread, 0.0), axis=0, keepdims=True))
    out[tile_rows * cols :, :] = jnp.concatenate(lines, axis=0).astype(jnp.bfloat16)


def in_vmem(*arrays):
    return [pltpu.with_memory_space_constraint(a, pltpu.VMEM) for a in arrays]


def profile_block(me, field, cross, near, stddev, diffusivity, columns, counts):
    tile_rows, cols, lev = stddev.shape
    vmem = pl.BlockSpec(memory_space=pltpu.VMEM)
    return pl.pallas_call(
        profile_kernel,
        out_shape=pltpu.VMEM((tile_rows * cols + QS, 2 * lev), jnp.bfloat16),
        in_specs=[pl.BlockSpec(memory_space=pltpu.SMEM)] + [vmem] * 7,
        out_specs=vmem,
        name="profile",
    )(me, *in_vmem(field, cross, near, stddev, diffusivity, columns, counts))


def band_columns(jac, offsets):
    band, ch = jac.shape

    def zeros(n):
        return jnp.zeros((n, ch), jac.dtype)

    x = jnp.concatenate([jac, zeros(8)], axis=0)
    for shift in (1, 2, 4):
        x = jnp.where((offsets & shift) != 0, pltpu.roll(x, shift, 0), x)
    for shift in (8, 16, 32):
        down = jnp.concatenate([zeros(shift), x], axis=0)
        stay = jnp.concatenate([x, zeros(shift)], axis=0)
        x = jnp.where((offsets & shift) != 0, down, stay)
    far = (offsets & 64) != 0
    top = jnp.where(far, zeros(64), x[:64])
    low = jnp.where(far, x[:64], jnp.concatenate([x[64:96], zeros(32)], axis=0))
    return jnp.concatenate([top, low], axis=0)


def respond_kernel(me_ref, gathered, jac, off, wts, mine, other, energy, sel, rows, adj):
    tiles, cells_ext, width = gathered.shape
    cells = sel.shape[1]
    sections = jac.shape[0]
    lev = width // 2
    slot = rows.shape[1] // sections
    me = me_ref[0]
    cell_id = lax.broadcasted_iota(jnp.int32, (cells, rows.shape[1]), 0).astype(jnp.float32)
    pick = lax.broadcasted_iota(jnp.int32, (tiles, width), 0) == me
    for q in range(tiles):
        block = gathered[q, cells : cells + tiles, :].astype(jnp.float32)
        target = jnp.sum(jnp.where(pick, block, 0.0), axis=0, keepdims=True)
        chosen = jnp.where(cell_id == target, 1.0, 0.0).astype(jnp.bfloat16)
        sel[q] = chosen
        rows[q] = lax.dot_general(
            chosen,
            gathered[q, :cells, :],
            (((0,), (0,)), ((), ())),
            preferred_element_type=jnp.float32,
        ).astype(jnp.bfloat16)
    for s in range(sections):
        row = pl.ds(s * tiles + me, 1)
        band = band_columns(jac[s].astype(jnp.float32), off[row, :]).astype(jnp.bfloat16)
        here = slice(s * slot, (s + 1) * slot)
        weight = wts[row, :]
        total = jnp.zeros((1, band.shape[1]), jnp.float32)
        for h in range(2):
            span = range(h * tiles // 2, (h + 1) * tiles // 2)
            mine_rows = jnp.concatenate(
                [rows[q, here, p * lev : (p + 1) * lev] for q in span for p in range(2)], axis=0
            )
            bright = jnp.dot(mine_rows, band, preferred_element_type=jnp.float32)
            weighted = weight * bright
            total = total + jnp.sum(bright * weighted, axis=0, keepdims=True)
            back = lax.dot_general(
                weighted.astype(jnp.bfloat16),
                band,
                (((1,), (1,)), ((), ())),
                preferred_element_type=jnp.float32,
            ).astype(jnp.bfloat16)
            at = 0
            for q in span:
                for p in range(2):
                    adj[q, here, p * lev : (p + 1) * lev] = back[at : at + slot]
                    at += slot
        each = energy.shape[0] // sections
        energy[s * each : (s + 1) * each] = jnp.broadcast_to(
            jnp.sum(total, axis=1, keepdims=True)[None], (each,) + energy.shape[1:]
        )
    for j in range(tiles // 2):
        for half, out in ((0, mine), (1, other)):
            q = ((me + 2 * j) & (tiles - 1)) if half == 0 else (((me ^ 1) + 2 * j) & (tiles - 1))
            out[j] = jnp.dot(sel[q], adj[q], preferred_element_type=jnp.float32)


def respond_all(me, gathered, jac, off, wts, copies):
    tiles, cells_ext, width = gathered.shape
    cells = cells_ext - tiles
    sections = jac.shape[0]
    part = pltpu.VMEM((tiles // 2, cells, width), jnp.float32)
    vmem = pl.BlockSpec(memory_space=pltpu.VMEM)
    return pl.pallas_call(
        respond_kernel,
        out_shape=(part, part, pltpu.VMEM((sections * copies, 4, 128), jnp.float32)),
        in_specs=[pl.BlockSpec(memory_space=pltpu.SMEM), vmem, vmem, vmem, vmem],
        out_specs=(vmem, vmem, vmem),
        scratch_shapes=[
            pltpu.VMEM((tiles, cells, 256), jnp.bfloat16),
            pltpu.VMEM((tiles, 256, width), jnp.bfloat16),
            pltpu.VMEM((tiles, 256, width), jnp.bfloat16),
        ],
        name="respond",
    )(me, *in_vmem(gathered, jac, off, wts))


def body(probes, stddev, diffusivity, counts, columns, jacobian, offsets, obs_weights):
    tile_count = lax.axis_size("tile")
    row_count, col_count, probe_count, levels = probes.shape
    slot_count = columns.shape[2]
    channels = jacobian.shape[1]
    cell_count = row_count * col_count
    sizes = (ZS, XS, CS)
    along_z = tile_groups(sizes, (0,))
    along_x = tile_groups(sizes, (1,))
    plane = tile_groups(sizes, (1, 2))
    here = lax.axis_index("tile")
    me = here & (QS - 1)
    cross, near = swap_edges(*edge_rows(probes, NSTEP))
    own = jnp.broadcast_to(jnp.swapaxes(jacobian, 1, 2), (ZS, jacobian.shape[2], channels))
    own, cross, near = lax.optimization_barrier((own, cross, near))
    jac = lax.all_to_all(
        own,
        "tile", 0, 0, axis_index_groups=along_z, tiled=True,
    )
    block = profile_block(
        me.reshape(1),
        probes.reshape(-1, levels),
        cross.reshape(-1, levels),
        near.reshape(-1, levels),
        stddev,
        diffusivity[None],
        columns[0].T,
        counts,
    )
    gathered = lax.all_gather(
        block[None],
        "tile", axis=0, axis_index_groups=plane, tiled=True,
    )
    lev_count = lax.axis_size("lev")
    mine, other, energy = respond_all(me.reshape(1), gathered, jac, offsets, obs_weights, lev_count)
    along_zy = [[t * lev_count + y for t in group for y in range(lev_count)] for group in along_z]
    shares = lax.all_to_all(energy, ("tile", "lev"), 0, 0, axis_index_groups=along_zy, tiled=True)
    summed = mine + lax.ppermute(other, "tile", [(i, i ^ 1) for i in range(tile_count)])
    gradient = summed[0]
    for step in range(1, XS):
        ring = [(i, i // QS * QS + (i + step * CS) % QS) for i in range(tile_count)]
        gradient = gradient + lax.ppermute(summed[step], "tile", ring)
    gradient = gradient.reshape(row_count, col_count, probe_count, levels)
    gradient, shares = lax.optimization_barrier((gradient, shares))
    trace_share = (
        jnp.sum(shares[:, 0, 0])
        * (1.0 / (probe_count * lev_count * tile_count * slot_count * channels))
    ).reshape(1)
    hessian = smooth(stddev[:, :, None, :] * gradient, diffusivity)
    return (hessian, trace_share)


def solution(mesh):
    placed = (
        P("tile", None, "lev", None),
        P("tile", None, None),
        P(),
        P("tile", None),
        P("tile", None, None),
        P("tile", None, None),
        P(),
        P(),
    )
    return jax.shard_map(
        body,
        mesh=mesh,
        in_specs=placed,
        out_specs=(P("tile", None, "lev", None), P("tile")),
        check_vma=False,
    )
```

```python
import jax
import jax.numpy as jnp
from jax import lax
from jax.experimental import pallas as pl
from jax.experimental.pallas import tpu as pltpu
from jax.sharding import PartitionSpec as P

NSTEP = 2
ZS, XS, CS = 16, 4, 2
QS = XS * CS
HALVING = (0, 3, 1, 2)


def tile_groups(sizes, free):
    groups = {}
    for z in range(sizes[0]):
        for x in range(sizes[1]):
            for c in range(sizes[2]):
                key = tuple(v for i, v in enumerate((z, x, c)) if i not in free)
                groups.setdefault(key, []).append((z * sizes[1] + x) * sizes[2] + c)
    return list(groups.values())


def laplace_step(ext, diffusivity):
    middle = ext[1:-1]
    padded = jnp.pad(middle, ((0, 0), (1, 1), (0, 0), (0, 0)))
    laplace = ext[2:] + ext[:-2] + padded[:, 2:] + padded[:, :-2] - 4.0 * middle
    return middle + diffusivity * laplace


def edge_rows(field, width):
    even = (lax.axis_index("tile") & 1) == 0
    top, bottom = field[:width], field[-width:]
    return jnp.where(even, top, bottom), jnp.where(even, bottom, top)


def swap_edges(to_cross, to_near):
    count = lax.axis_size("tile")
    across = [(i, (i - 1 if i % 2 == 0 else i + 1) % count) for i in range(count)]
    cross = lax.ppermute(to_cross, "tile", across)
    near = lax.ppermute(to_near, "tile", [(i, i ^ 1) for i in range(count)])
    return cross, near


def smooth(field, edges, diffusivity):
    cross, near = edges
    even = (lax.axis_index("tile") & 1) == 0
    ext = jnp.concatenate(
        [jnp.where(even, cross, near), field, jnp.where(even, near, cross)], axis=0
    )
    for _ in range(NSTEP):
        ext = laplace_step(ext, diffusivity)
    return ext


def target_kernel(columns, counts, probes, stddev, out, field, spread):
    field[...] = probes[...].astype(jnp.float32)
    spread[...] = stddev[...]
    slots, sections = columns.shape
    width = out.shape[1]
    live = lax.broadcasted_iota(jnp.int32, (slots, sections), 0) < counts[...]
    target = jnp.where(live, columns[...], -1).astype(jnp.float32).astype(jnp.bfloat16)
    lane = lax.broadcasted_iota(jnp.int32, (sections, width), 1)
    apart = lax.broadcasted_iota(jnp.int32, (sections, width), 0) - (lane >> 4) * QS
    slot = lax.broadcasted_iota(jnp.int32, (slots, width), 0)
    mine = slot == (lax.broadcasted_iota(jnp.int32, (slots, width), 1) & (slots - 1))
    lines = []
    for q in range(QS):
        choose = jnp.where(apart == q, 1.0, 0.0).astype(jnp.bfloat16)
        spread = jnp.dot(target, choose, preferred_element_type=jnp.float32)
        lines.append(jnp.sum(jnp.where(mine, spread, 0.0), axis=0, keepdims=True))
    out[...] = jnp.concatenate(lines, axis=0).astype(jnp.bfloat16)


def in_vmem(*arrays):
    return [pltpu.with_memory_space_constraint(a, pltpu.VMEM) for a in arrays]


def slot_targets(columns, counts, probes, stddev):
    vmem = pl.BlockSpec(memory_space=pltpu.VMEM)
    return pl.pallas_call(
        target_kernel,
        out_shape=(
            pltpu.VMEM((QS, columns.size // QS), jnp.bfloat16),
            pltpu.VMEM(probes.shape, jnp.float32),
            pltpu.VMEM(stddev.shape, jnp.float32),
        ),
        in_specs=[vmem] * 4,
        out_specs=(vmem, vmem, vmem),
        name="targets",
    )(*in_vmem(columns, counts, probes, stddev))


def band_columns(jac, offsets):
    band, ch = jac.shape

    def zeros(n):
        return jnp.zeros((n, ch), jac.dtype)

    x = jnp.concatenate([jac, zeros(8)], axis=0)
    for shift in (1, 2, 4):
        x = jnp.where((offsets & shift) != 0, pltpu.roll(x, shift, 0), x)
    for shift in (8, 16, 32):
        down = jnp.concatenate([zeros(shift), x], axis=0)
        stay = jnp.concatenate([x, zeros(shift)], axis=0)
        x = jnp.where((offsets & shift) != 0, down, stay)
    far = (offsets & 64) != 0
    top = jnp.where(far, zeros(64), x[:64])
    low = jnp.where(far, x[:64], jnp.concatenate([x[64:96], zeros(32)], axis=0))
    return jnp.concatenate([top, low], axis=0)


def respond_kernel(me_ref, gathered, jac, off, wts, mine, other, energy, sel, rows, adj):
    tiles, cells_ext, width = gathered.shape
    cells = sel.shape[1]
    sections = jac.shape[0]
    lev = width // 2
    slot = rows.shape[1] // sections
    me = me_ref[0]
    cell_id = lax.broadcasted_iota(jnp.int32, (cells, rows.shape[1]), 0).astype(jnp.float32)
    pick = lax.broadcasted_iota(jnp.int32, (tiles, width), 0) == me
    for q in range(tiles):
        block = gathered[q, cells : cells + tiles, :].astype(jnp.float32)
        target = jnp.sum(jnp.where(pick, block, 0.0), axis=0, keepdims=True)
        chosen = jnp.where(cell_id == target, 1.0, 0.0).astype(jnp.bfloat16)
        sel[q] = chosen
        rows[q] = lax.dot_general(
            chosen,
            gathered[q, :cells, :],
            (((0,), (0,)), ((), ())),
            preferred_element_type=jnp.float32,
        ).astype(jnp.bfloat16)
    for s in range(sections):
        row = pl.ds(s * tiles + me, 1)
        band = band_columns(jac[s].astype(jnp.float32), off[row, :]).astype(jnp.bfloat16)
        here = slice(s * slot, (s + 1) * slot)
        weight = wts[row, :]
        total = jnp.zeros((1, band.shape[1]), jnp.float32)
        for h in range(2):
            span = range(h * tiles // 2, (h + 1) * tiles // 2)
            mine_rows = jnp.concatenate(
                [rows[q, here, p * lev : (p + 1) * lev] for q in span for p in range(2)], axis=0
            )
            bright = jnp.dot(mine_rows, band, preferred_element_type=jnp.float32)
            weighted = weight * bright
            total = total + jnp.sum(bright * weighted, axis=0, keepdims=True)
            back = lax.dot_general(
                weighted.astype(jnp.bfloat16),
                band,
                (((1,), (1,)), ((), ())),
                preferred_element_type=jnp.float32,
            ).astype(jnp.bfloat16)
            at = 0
            for q in span:
                for p in range(2):
                    adj[q, here, p * lev : (p + 1) * lev] = back[at : at + slot]
                    at += slot
        each = energy.shape[0] // sections
        energy[s * each : (s + 1) * each] = jnp.broadcast_to(
            jnp.sum(total, axis=1, keepdims=True)[None], (each,) + energy.shape[1:]
        )
    for j, away in enumerate(HALVING):
        for half, out in ((0, mine), (1, other)):
            q = me ^ (CS * away + half)
            out[j] = jnp.dot(sel[q], adj[q], preferred_element_type=jnp.float32)


def respond_all(me, gathered, jac, off, wts, copies):
    tiles, cells_ext, width = gathered.shape
    cells = cells_ext - tiles
    sections = jac.shape[0]
    part = pltpu.VMEM((tiles // 2, cells, width), jnp.float32)
    vmem = pl.BlockSpec(memory_space=pltpu.VMEM)
    return pl.pallas_call(
        respond_kernel,
        out_shape=(part, part, pltpu.VMEM((sections * copies, 1, 128), jnp.float32)),
        in_specs=[pl.BlockSpec(memory_space=pltpu.SMEM), vmem, vmem, vmem, vmem],
        out_specs=(vmem, vmem, vmem),
        scratch_shapes=[
            pltpu.VMEM((tiles, cells, 256), jnp.bfloat16),
            pltpu.VMEM((tiles, 256, width), jnp.bfloat16),
            pltpu.VMEM((tiles, 256, width), jnp.bfloat16),
        ],
        name="respond",
    )(me, *in_vmem(gathered, jac, off, wts))


def body(probes, stddev, diffusivity, counts, columns, jacobian, offsets, obs_weights):
    tile_count = lax.axis_size("tile")
    row_count, col_count, probe_count, levels = probes.shape
    slot_count = columns.shape[2]
    channels = jacobian.shape[1]
    cell_count = row_count * col_count
    sizes = (ZS, XS, CS)
    along_z = tile_groups(sizes, (0,))
    along_x = tile_groups(sizes, (1,))
    plane = tile_groups(sizes, (1, 2))
    here = lax.axis_index("tile")
    me = here & (QS - 1)
    starts, own = lax.optimization_barrier((edge_rows(probes, NSTEP), jnp.swapaxes(jacobian, 1, 2)))
    jac = lax.all_to_all(
        jnp.broadcast_to(own, (ZS,) + own.shape[1:]),
        "tile", 0, 0, axis_index_groups=along_z, tiled=True,
    )
    cross, near = swap_edges(*starts)
    targets, field, spread = slot_targets(
        columns[0].T, counts, probes.reshape(-1, levels), stddev
    )
    even = (me & 1) == 0
    ext = jnp.concatenate(
        [
            jnp.where(even, cross, near).astype(jnp.float32),
            field.reshape(probes.shape),
            jnp.where(even, near, cross).astype(jnp.float32),
        ],
        axis=0,
    )
    for _ in range(NSTEP):
        ext = laplace_step(ext, diffusivity)
    profile = (spread[:, :, None, :] * ext).astype(jnp.bfloat16)
    block = jnp.concatenate([profile.reshape(cell_count, -1), targets], axis=0)
    gathered = lax.all_gather(
        block[None],
        "tile", axis=0, axis_index_groups=plane, tiled=True,
    )
    lev_count = lax.axis_size("lev")
    mine, other, energy = respond_all(me.reshape(1), gathered, jac, offsets, obs_weights, lev_count)
    along_zy = [[t * lev_count + y for t in group for y in range(lev_count)] for group in along_z]
    shares = lax.all_to_all(energy, ("tile", "lev"), 0, 0, axis_index_groups=along_zy, tiled=True)
    summed = mine + lax.ppermute(other, "tile", [(i, i ^ 1) for i in range(tile_count)])
    x = here >> 1
    pairs = [[t, t + CS] for t in range(tile_count) if (t >> 1) & 1 == 0]
    sent = lax.all_gather(summed[2:], "tile", axis=0, axis_index_groups=pairs)
    halves = summed[:2] + lax.dynamic_index_in_dim(sent, 1 - (x & 1), 0, keepdims=False)
    pairs = [[t, t ^ (3 * CS)] for t in range(tile_count) if (t >> 1) & 2 == 0]
    sent = lax.all_gather(halves[1], "tile", axis=0, axis_index_groups=pairs)
    gradient = halves[0] + lax.dynamic_index_in_dim(sent, 1 - ((x >> 1) & 1), 0, keepdims=False)
    gradient = gradient.reshape(row_count, col_count, probe_count, levels)
    scaled = stddev[:, :, None, :] * gradient
    edges = swap_edges(*edge_rows(scaled, NSTEP))
    trace_share = (
        jnp.sum(shares[:, 0, 0])
        * (1.0 / (probe_count * lev_count * tile_count * slot_count * channels))
    ).reshape(1)
    edges, trace_share = lax.optimization_barrier((edges, trace_share))
    hessian = smooth(scaled, edges, diffusivity)
    return (hessian, trace_share)


def solution(mesh):
    placed = (
        P("tile", None, "lev", None),
        P("tile", None, None),
        P(),
        P("tile", None),
        P("tile", None, None),
        P("tile", None, None),
        P(),
        P(),
    )
    return jax.shard_map(
        body,
        mesh=mesh,
        in_specs=placed,
        out_specs=(P("tile", None, "lev", None), P("tile")),
        check_vma=False,
    )
```

```python
import jax
import jax.numpy as jnp
from jax import lax
from jax.experimental import pallas as pl
from jax.experimental.pallas import tpu as pltpu
from jax.sharding import PartitionSpec as P

NSTEP = 2
ZS, XS, CS = 16, 4, 2
QS = XS * CS
HALVING = (0, 3, 1, 2)


def tile_groups(sizes, free):
    groups = {}
    for z in range(sizes[0]):
        for x in range(sizes[1]):
            for c in range(sizes[2]):
                key = tuple(v for i, v in enumerate((z, x, c)) if i not in free)
                groups.setdefault(key, []).append((z * sizes[1] + x) * sizes[2] + c)
    return list(groups.values())


def laplace_step(ext, diffusivity):
    middle = ext[1:-1]
    padded = jnp.pad(middle, ((0, 0), (1, 1), (0, 0), (0, 0)))
    laplace = ext[2:] + ext[:-2] + padded[:, 2:] + padded[:, :-2] - 4.0 * middle
    return middle + diffusivity * laplace


def edge_rows(field, width):
    even = (lax.axis_index("tile") & 1) == 0
    top, bottom = field[:width], field[-width:]
    return jnp.where(even, top, bottom), jnp.where(even, bottom, top)


def cross_pairs(count):
    return [(i, (i - 1 if i % 2 == 0 else i + 1) % count) for i in range(count)]


def swap_edges(to_cross, to_near):
    count = lax.axis_size("tile")
    cross = lax.ppermute(to_cross, "tile", cross_pairs(count))
    near = lax.ppermute(to_near, "tile", [(i, i ^ 1) for i in range(count)])
    return cross, near


def smooth(field, edges, diffusivity):
    cross, near = edges
    even = (lax.axis_index("tile") & 1) == 0
    ext = jnp.concatenate(
        [jnp.where(even, cross, near), field, jnp.where(even, near, cross)], axis=0
    )
    for _ in range(NSTEP):
        ext = laplace_step(ext, diffusivity)
    return ext


def in_vmem(*arrays):
    return [pltpu.with_memory_space_constraint(a, pltpu.VMEM) for a in arrays]


def stage_kernel(
    me_ref, probes, jac, stddev, diffusivity, columns, counts,
    to_cross, to_near, copies, field, spread, rate, out,
):
    edge = to_cross.shape[0]
    even = (me_ref[0] & 1) == 0
    top, bottom = probes[:edge], probes[-edge:]
    to_cross[...] = jnp.where(even, top, bottom)
    to_near[...] = jnp.where(even, bottom, top)
    for z in range(copies.shape[0]):
        copies[z] = jac[...]
    field[...] = probes[...].astype(jnp.float32)
    spread[...] = stddev[...]
    rate[...] = diffusivity[...]
    slots, sections = columns.shape
    width = out.shape[1]
    live = lax.broadcasted_iota(jnp.int32, (slots, sections), 0) < counts[...]
    target = jnp.where(live, columns[...], -1).astype(jnp.float32).astype(jnp.bfloat16)
    lane = lax.broadcasted_iota(jnp.int32, (sections, width), 1)
    apart = lax.broadcasted_iota(jnp.int32, (sections, width), 0) - (lane >> 4) * QS
    slot = lax.broadcasted_iota(jnp.int32, (slots, width), 0)
    mine = slot == (lax.broadcasted_iota(jnp.int32, (slots, width), 1) & (slots - 1))
    lines = []
    for q in range(QS):
        choose = jnp.where(apart == q, 1.0, 0.0).astype(jnp.bfloat16)
        spread = jnp.dot(target, choose, preferred_element_type=jnp.float32)
        lines.append(jnp.sum(jnp.where(mine, spread, 0.0), axis=0, keepdims=True))
    out[...] = jnp.concatenate(lines, axis=0).astype(jnp.bfloat16)


def stage(me, probes, jac, stddev, diffusivity, columns, counts, edge):
    vmem = pl.BlockSpec(memory_space=pltpu.VMEM)
    rows = pltpu.VMEM((edge, probes.shape[1]), probes.dtype)
    return pl.pallas_call(
        stage_kernel,
        out_shape=(
            rows,
            rows,
            jax.ShapeDtypeStruct((ZS,) + jac.shape, jac.dtype),
            pltpu.VMEM(probes.shape, jnp.float32),
            pltpu.VMEM(stddev.shape, jnp.float32),
            pltpu.VMEM(diffusivity.shape, jnp.float32),
            pltpu.VMEM((QS, columns.size // QS), jnp.bfloat16),
        ),
        in_specs=[pl.BlockSpec(memory_space=pltpu.SMEM)] + [vmem] * 6,
        out_specs=(vmem,) * 7,
        name="stage",
    )(me, probes, jac, stddev, diffusivity, columns, counts)


def band_columns(jac, offsets):
    band, ch = jac.shape

    def zeros(n):
        return jnp.zeros((n, ch), jac.dtype)

    x = jnp.concatenate([jac, zeros(8)], axis=0)
    for shift in (1, 2, 4):
        x = jnp.where((offsets & shift) != 0, pltpu.roll(x, shift, 0), x)
    for shift in (8, 16, 32):
        down = jnp.concatenate([zeros(shift), x], axis=0)
        stay = jnp.concatenate([x, zeros(shift)], axis=0)
        x = jnp.where((offsets & shift) != 0, down, stay)
    far = (offsets & 64) != 0
    top = jnp.where(far, zeros(64), x[:64])
    low = jnp.where(far, x[:64], jnp.concatenate([x[64:96], zeros(32)], axis=0))
    return jnp.concatenate([top, low], axis=0)


def respond_kernel(me_ref, gathered, jac, off, wts, mine, other, energy, sel, rows, adj):
    tiles, cells_ext, width = gathered.shape
    cells = sel.shape[1]
    sections = jac.shape[0]
    lev = width // 2
    slot = rows.shape[1] // sections
    me = me_ref[0]
    cell_id = lax.broadcasted_iota(jnp.int32, (cells, rows.shape[1]), 0).astype(jnp.float32)
    pick = lax.broadcasted_iota(jnp.int32, (tiles, width), 0) == me
    for q in range(tiles):
        block = gathered[q, cells : cells + tiles, :].astype(jnp.float32)
        target = jnp.sum(jnp.where(pick, block, 0.0), axis=0, keepdims=True)
        chosen = jnp.where(cell_id == target, 1.0, 0.0).astype(jnp.bfloat16)
        sel[q] = chosen
        rows[q] = lax.dot_general(
            chosen,
            gathered[q, :cells, :],
            (((0,), (0,)), ((), ())),
            preferred_element_type=jnp.float32,
        ).astype(jnp.bfloat16)
    for s in range(sections):
        row = pl.ds(s * tiles + me, 1)
        band = band_columns(jac[s].astype(jnp.float32), off[row, :]).astype(jnp.bfloat16)
        here = slice(s * slot, (s + 1) * slot)
        weight = wts[row, :]
        total = jnp.zeros((1, band.shape[1]), jnp.float32)
        for h in range(2):
            span = range(h * tiles // 2, (h + 1) * tiles // 2)
            mine_rows = jnp.concatenate(
                [rows[q, here, p * lev : (p + 1) * lev] for q in span for p in range(2)], axis=0
            )
            bright = jnp.dot(mine_rows, band, preferred_element_type=jnp.float32)
            weighted = weight * bright
            total = total + jnp.sum(bright * weighted, axis=0, keepdims=True)
            back = lax.dot_general(
                weighted.astype(jnp.bfloat16),
                band,
                (((1,), (1,)), ((), ())),
                preferred_element_type=jnp.float32,
            ).astype(jnp.bfloat16)
            at = 0
            for q in span:
                for p in range(2):
                    adj[q, here, p * lev : (p + 1) * lev] = back[at : at + slot]
                    at += slot
        each = energy.shape[0] // sections
        energy[s * each : (s + 1) * each] = jnp.broadcast_to(
            jnp.sum(total, axis=1, keepdims=True)[None], (each,) + energy.shape[1:]
        )
    for j, away in enumerate(HALVING):
        for half, out in ((0, mine), (1, other)):
            q = me ^ (CS * away + half)
            out[j] = jnp.dot(sel[q], adj[q], preferred_element_type=jnp.float32)


def respond_all(me, gathered, jac, off, wts, copies):
    tiles, cells_ext, width = gathered.shape
    cells = cells_ext - tiles
    sections = jac.shape[0]
    part = pltpu.VMEM((tiles // 2, cells, width), jnp.float32)
    vmem = pl.BlockSpec(memory_space=pltpu.VMEM)
    return pl.pallas_call(
        respond_kernel,
        out_shape=(part, part, pltpu.VMEM((sections * copies, 1, 128), jnp.float32)),
        in_specs=[pl.BlockSpec(memory_space=pltpu.SMEM), vmem, vmem, vmem, vmem],
        out_specs=(vmem, vmem, vmem),
        scratch_shapes=[
            pltpu.VMEM((tiles, cells, 256), jnp.bfloat16),
            pltpu.VMEM((tiles, 256, width), jnp.bfloat16),
            pltpu.VMEM((tiles, 256, width), jnp.bfloat16),
        ],
        name="respond",
    )(me, *in_vmem(gathered, jac, off, wts))


def body(probes, stddev, diffusivity, counts, columns, jacobian, offsets, obs_weights):
    tile_count = lax.axis_size("tile")
    row_count, col_count, probe_count, levels = probes.shape
    slot_count = columns.shape[2]
    channels = jacobian.shape[1]
    cell_count = row_count * col_count
    sizes = (ZS, XS, CS)
    along_z = tile_groups(sizes, (0,))
    along_x = tile_groups(sizes, (1,))
    plane = tile_groups(sizes, (1, 2))
    here = lax.axis_index("tile")
    me = here & (QS - 1)
    to_cross, to_near, copies, field, spread, rate, targets = stage(
        me.reshape(1), probes.reshape(-1, levels), jacobian[0].T, stddev, diffusivity[None],
        columns[0].T, counts, NSTEP * col_count * probe_count,
    )
    jac = lax.all_to_all(copies, "tile", 0, 0, axis_index_groups=along_z, tiled=True)
    rows = (NSTEP, col_count, probe_count, levels)
    cross = lax.ppermute(to_cross, "tile", cross_pairs(tile_count))
    to_near, cross = lax.optimization_barrier((to_near, cross))
    near = lax.all_gather(
        to_near, "tile", axis=0, axis_index_groups=tile_groups(sizes, (2,)),
    )
    near = lax.dynamic_index_in_dim(near, 1 - (me & 1), 0, keepdims=False)
    cross, near = cross.reshape(rows), near.reshape(rows)
    even = (me & 1) == 0
    ext = jnp.concatenate(
        [
            jnp.where(even, cross, near).astype(jnp.float32),
            field.reshape(probes.shape),
            jnp.where(even, near, cross).astype(jnp.float32),
        ],
        axis=0,
    )
    for _ in range(NSTEP):
        ext = laplace_step(ext, rate[0])
    profile = (spread[:, :, None, :] * ext).astype(jnp.bfloat16)
    block = jnp.concatenate([profile.reshape(cell_count, -1), targets], axis=0)
    gathered = lax.all_gather(
        block[None],
        "tile", axis=0, axis_index_groups=plane, tiled=True,
    )
    lev_count = lax.axis_size("lev")
    mine, other, energy = respond_all(me.reshape(1), gathered, jac, offsets, obs_weights, lev_count)
    along_zy = [[t * lev_count + y for t in group for y in range(lev_count)] for group in along_z]
    shares = lax.all_to_all(energy, ("tile", "lev"), 0, 0, axis_index_groups=along_zy, tiled=True)
    summed = mine + lax.ppermute(other, "tile", [(i, i ^ 1) for i in range(tile_count)])
    x = here >> 1
    pairs = [[t, t + CS] for t in range(tile_count) if (t >> 1) & 1 == 0]
    sent = lax.all_gather(summed[2:], "tile", axis=0, axis_index_groups=pairs)
    halves = summed[:2] + lax.dynamic_index_in_dim(sent, 1 - (x & 1), 0, keepdims=False)
    pairs = [[t, t ^ (3 * CS)] for t in range(tile_count) if (t >> 1) & 2 == 0]
    sent = lax.all_gather(halves[1], "tile", axis=0, axis_index_groups=pairs)
    gradient = halves[0] + lax.dynamic_index_in_dim(sent, 1 - ((x >> 1) & 1), 0, keepdims=False)
    gradient = gradient.reshape(row_count, col_count, probe_count, levels)
    scaled = spread[:, :, None, :] * gradient
    edges = swap_edges(*edge_rows(scaled, NSTEP))
    trace_share = (
        jnp.sum(shares[:, 0, 0])
        * (1.0 / (probe_count * lev_count * tile_count * slot_count * channels))
    ).reshape(1)
    edges, trace_share = lax.optimization_barrier((edges, trace_share))
    hessian = smooth(scaled, edges, rate[0])
    return (hessian, trace_share)


def solution(mesh):
    placed = (
        P("tile", None, "lev", None),
        P("tile", None, None),
        P(),
        P("tile", None),
        P("tile", None, None),
        P("tile", None, None),
        P(),
        P(),
    )
    return jax.shard_map(
        body,
        mesh=mesh,
        in_specs=placed,
        out_specs=(P("tile", None, "lev", None), P("tile")),
        check_vma=False,
    )
```

```python
import jax
import jax.numpy as jnp
from jax import lax
from jax.experimental import pallas as pl
from jax.experimental.pallas import tpu as pltpu
from jax.sharding import PartitionSpec as P

NSTEP = 2
ZS, XS, CS = 16, 4, 2
QS = XS * CS
HALVING = (0, 3, 1, 2)


def tile_groups(sizes, free):
    groups = {}
    for z in range(sizes[0]):
        for x in range(sizes[1]):
            for c in range(sizes[2]):
                key = tuple(v for i, v in enumerate((z, x, c)) if i not in free)
                groups.setdefault(key, []).append((z * sizes[1] + x) * sizes[2] + c)
    return list(groups.values())


def laplace_step(ext, diffusivity):
    middle = ext[1:-1]
    padded = jnp.pad(middle, ((0, 0), (1, 1), (0, 0), (0, 0)))
    laplace = ext[2:] + ext[:-2] + padded[:, 2:] + padded[:, :-2] - 4.0 * middle
    return middle + diffusivity * laplace


def edge_rows(field, width):
    even = (lax.axis_index("tile") & 1) == 0
    top, bottom = field[:width], field[-width:]
    return jnp.where(even, top, bottom), jnp.where(even, bottom, top)


def cross_pairs(count):
    return [(i, (i - 1 if i % 2 == 0 else i + 1) % count) for i in range(count)]


def swap_edges(to_cross, to_near):
    count = lax.axis_size("tile")
    cross = lax.ppermute(to_cross, "tile", cross_pairs(count))
    near = lax.ppermute(to_near, "tile", [(i, i ^ 1) for i in range(count)])
    return cross, near


def in_vmem(*arrays):
    return [pltpu.with_memory_space_constraint(a, pltpu.VMEM) for a in arrays]


def stage_kernel(
    me_ref, probes, jac, stddev, diffusivity, columns, counts,
    to_cross, to_near, copies, field, spread, rate, out,
):
    edge = to_cross.shape[0]
    even = (me_ref[0] & 1) == 0
    top, bottom = probes[:edge], probes[-edge:]
    to_cross[...] = jnp.where(even, top, bottom)
    to_near[...] = jnp.where(even, bottom, top)
    for z in range(copies.shape[0]):
        copies[z] = jac[...]
    field[...] = probes[...].astype(jnp.float32)
    spread[...] = stddev[...]
    rate[...] = diffusivity[...]
    slots, sections = columns.shape
    width = out.shape[1]
    live = lax.broadcasted_iota(jnp.int32, (slots, sections), 0) < counts[...]
    target = jnp.where(live, columns[...], -1).astype(jnp.float32).astype(jnp.bfloat16)
    lane = lax.broadcasted_iota(jnp.int32, (sections, width), 1)
    apart = lax.broadcasted_iota(jnp.int32, (sections, width), 0) - (lane >> 4) * QS
    slot = lax.broadcasted_iota(jnp.int32, (slots, width), 0)
    mine = slot == (lax.broadcasted_iota(jnp.int32, (slots, width), 1) & (slots - 1))
    lines = []
    for q in range(QS):
        choose = jnp.where(apart == q, 1.0, 0.0).astype(jnp.bfloat16)
        spread = jnp.dot(target, choose, preferred_element_type=jnp.float32)
        lines.append(jnp.sum(jnp.where(mine, spread, 0.0), axis=0, keepdims=True))
    out[...] = jnp.concatenate(lines, axis=0).astype(jnp.bfloat16)


def stage(me, probes, jac, stddev, diffusivity, columns, counts, edge):
    vmem = pl.BlockSpec(memory_space=pltpu.VMEM)
    rows = pltpu.VMEM((edge, probes.shape[1]), probes.dtype)
    return pl.pallas_call(
        stage_kernel,
        out_shape=(
            rows,
            rows,
            jax.ShapeDtypeStruct((ZS,) + jac.shape, jac.dtype),
            pltpu.VMEM(probes.shape, jnp.float32),
            pltpu.VMEM(stddev.shape, jnp.float32),
            pltpu.VMEM(diffusivity.shape, jnp.float32),
            pltpu.VMEM((QS, columns.size // QS), jnp.bfloat16),
        ),
        in_specs=[pl.BlockSpec(memory_space=pltpu.SMEM)] + [vmem] * 6,
        out_specs=(vmem,) * 7,
        name="stage",
    )(me, probes, jac, stddev, diffusivity, columns, counts)


def spread_kernel(me_ref, scaled, cross, near, rate, out):
    wide = cross.shape[0] // NSTEP
    even = (me_ref[0] & 1) == 0
    before = jnp.where(even, cross[...], near[...])
    after = jnp.where(even, near[...], cross[...])
    tile = scaled[...]
    grid = [b[i : i + wide] for b in (before, tile, after) for i in range(0, b.shape[0], wide)]
    place = lax.broadcasted_iota(jnp.int32, (wide, scaled.shape[1]), 0)
    speed = rate[...]
    for _ in range(NSTEP):
        new = []
        for i in range(1, len(grid) - 1):
            middle = grid[i]
            following = jnp.where(place >= wide - 2, 0.0, pltpu.roll(middle, wide - 2, 0))
            leading = jnp.where(place < 2, 0.0, pltpu.roll(middle, 2, 0))
            laplace = grid[i + 1] + grid[i - 1] + following + leading - 4.0 * middle
            new.append(middle + speed * laplace)
        grid = new
    for i, row in enumerate(grid):
        out[i * wide : (i + 1) * wide] = row


def spread_tile(me, scaled, cross, near, rate):
    vmem = pl.BlockSpec(memory_space=pltpu.VMEM)
    return pl.pallas_call(
        spread_kernel,
        out_shape=jax.ShapeDtypeStruct(scaled.shape, jnp.float32),
        in_specs=[pl.BlockSpec(memory_space=pltpu.SMEM)] + [vmem] * 4,
        out_specs=vmem,
        name="diffuse",
    )(me, *in_vmem(scaled, cross, near, rate))


def band_columns(jac, offsets):
    band, ch = jac.shape

    def zeros(n):
        return jnp.zeros((n, ch), jac.dtype)

    x = jnp.concatenate([jac, zeros(8)], axis=0)
    for shift in (1, 2, 4):
        x = jnp.where((offsets & shift) != 0, pltpu.roll(x, shift, 0), x)
    for shift in (8, 16, 32):
        down = jnp.concatenate([zeros(shift), x], axis=0)
        stay = jnp.concatenate([x, zeros(shift)], axis=0)
        x = jnp.where((offsets & shift) != 0, down, stay)
    far = (offsets & 64) != 0
    top = jnp.where(far, zeros(64), x[:64])
    low = jnp.where(far, x[:64], jnp.concatenate([x[64:96], zeros(32)], axis=0))
    return jnp.concatenate([top, low], axis=0)


def respond_kernel(me_ref, gathered, jac, off, wts, mine, other, energy, sel, rows, adj):
    tiles, cells_ext, width = gathered.shape
    cells = sel.shape[1]
    sections = jac.shape[0]
    lev = width // 2
    slot = rows.shape[1] // sections
    me = me_ref[0]
    cell_id = lax.broadcasted_iota(jnp.int32, (cells, rows.shape[1]), 0).astype(jnp.float32)
    pick = lax.broadcasted_iota(jnp.int32, (tiles, width), 0) == me
    for q in range(tiles):
        block = gathered[q, cells : cells + tiles, :].astype(jnp.float32)
        target = jnp.sum(jnp.where(pick, block, 0.0), axis=0, keepdims=True)
        chosen = jnp.where(cell_id == target, 1.0, 0.0).astype(jnp.bfloat16)
        sel[q] = chosen
        rows[q] = lax.dot_general(
            chosen,
            gathered[q, :cells, :],
            (((0,), (0,)), ((), ())),
            preferred_element_type=jnp.float32,
        ).astype(jnp.bfloat16)
    for s in range(sections):
        row = pl.ds(s * tiles + me, 1)
        band = band_columns(jac[s].astype(jnp.float32), off[row, :]).astype(jnp.bfloat16)
        here = slice(s * slot, (s + 1) * slot)
        weight = wts[row, :]
        total = jnp.zeros((1, band.shape[1]), jnp.float32)
        for h in range(2):
            span = range(h * tiles // 2, (h + 1) * tiles // 2)
            mine_rows = jnp.concatenate(
                [rows[q, here, p * lev : (p + 1) * lev] for q in span for p in range(2)], axis=0
            )
            bright = jnp.dot(mine_rows, band, preferred_element_type=jnp.float32)
            weighted = weight * bright
            total = total + jnp.sum(bright * weighted, axis=0, keepdims=True)
            back = lax.dot_general(
                weighted.astype(jnp.bfloat16),
                band,
                (((1,), (1,)), ((), ())),
                preferred_element_type=jnp.float32,
            ).astype(jnp.bfloat16)
            at = 0
            for q in span:
                for p in range(2):
                    adj[q, here, p * lev : (p + 1) * lev] = back[at : at + slot]
                    at += slot
        each = energy.shape[0] // sections
        energy[s * each : (s + 1) * each] = jnp.broadcast_to(
            jnp.sum(total, axis=1, keepdims=True)[None], (each,) + energy.shape[1:]
        )
    for j, away in enumerate(HALVING):
        for half, out in ((0, mine), (1, other)):
            q = me ^ (CS * away + half)
            out[j] = jnp.dot(sel[q], adj[q], preferred_element_type=jnp.float32)


def respond_all(me, gathered, jac, off, wts, copies):
    tiles, cells_ext, width = gathered.shape
    cells = cells_ext - tiles
    sections = jac.shape[0]
    part = pltpu.VMEM((tiles // 2, cells, width), jnp.float32)
    vmem = pl.BlockSpec(memory_space=pltpu.VMEM)
    return pl.pallas_call(
        respond_kernel,
        out_shape=(part, part, pltpu.VMEM((sections * copies, 1, 128), jnp.float32)),
        in_specs=[pl.BlockSpec(memory_space=pltpu.SMEM), vmem, vmem, vmem, vmem],
        out_specs=(vmem, vmem, vmem),
        scratch_shapes=[
            pltpu.VMEM((tiles, cells, 256), jnp.bfloat16),
            pltpu.VMEM((tiles, 256, width), jnp.bfloat16),
            pltpu.VMEM((tiles, 256, width), jnp.bfloat16),
        ],
        name="respond",
    )(me, *in_vmem(gathered, jac, off, wts))


def body(probes, stddev, diffusivity, counts, columns, jacobian, offsets, obs_weights):
    tile_count = lax.axis_size("tile")
    row_count, col_count, probe_count, levels = probes.shape
    slot_count = columns.shape[2]
    channels = jacobian.shape[1]
    cell_count = row_count * col_count
    sizes = (ZS, XS, CS)
    along_z = tile_groups(sizes, (0,))
    along_x = tile_groups(sizes, (1,))
    plane = tile_groups(sizes, (1, 2))
    here = lax.axis_index("tile")
    me = here & (QS - 1)
    to_cross, to_near, copies, field, spread, rate, targets = stage(
        me.reshape(1), probes.reshape(-1, levels), jacobian[0].T, stddev, diffusivity[None],
        columns[0].T, counts, NSTEP * col_count * probe_count,
    )
    jac = lax.all_to_all(copies, "tile", 0, 0, axis_index_groups=along_z, tiled=True)
    rows = (NSTEP, col_count, probe_count, levels)
    cross = lax.ppermute(to_cross, "tile", cross_pairs(tile_count))
    to_near, cross = lax.optimization_barrier((to_near, cross))
    near = lax.all_gather(
        to_near, "tile", axis=0, axis_index_groups=tile_groups(sizes, (2,)),
    )
    near = lax.dynamic_index_in_dim(near, 1 - (me & 1), 0, keepdims=False)
    cross, near = cross.reshape(rows), near.reshape(rows)
    even = (me & 1) == 0
    ext = jnp.concatenate(
        [
            jnp.where(even, cross, near).astype(jnp.float32),
            field.reshape(probes.shape),
            jnp.where(even, near, cross).astype(jnp.float32),
        ],
        axis=0,
    )
    for _ in range(NSTEP):
        ext = laplace_step(ext, rate[0])
    profile = (spread[:, :, None, :] * ext).astype(jnp.bfloat16)
    block = jnp.concatenate([profile.reshape(cell_count, -1), targets], axis=0)
    gathered = lax.all_gather(
        block[None],
        "tile", axis=0, axis_index_groups=plane, tiled=True,
    )
    lev_count = lax.axis_size("lev")
    mine, other, energy = respond_all(me.reshape(1), gathered, jac, offsets, obs_weights, lev_count)
    along_zy = [[t * lev_count + y for t in group for y in range(lev_count)] for group in along_z]
    shares = lax.all_to_all(energy, ("tile", "lev"), 0, 0, axis_index_groups=along_zy, tiled=True)
    summed = mine + lax.ppermute(other, "tile", [(i, i ^ 1) for i in range(tile_count)])
    x = here >> 1
    pairs = [[t, t + CS] for t in range(tile_count) if (t >> 1) & 1 == 0]
    sent = lax.all_gather(summed[2:], "tile", axis=0, axis_index_groups=pairs)
    halves = summed[:2] + lax.dynamic_index_in_dim(sent, 1 - (x & 1), 0, keepdims=False)
    pairs = [[t, t ^ (3 * CS)] for t in range(tile_count) if (t >> 1) & 2 == 0]
    sent = lax.all_gather(halves[1], "tile", axis=0, axis_index_groups=pairs)
    gradient = halves[0] + lax.dynamic_index_in_dim(sent, 1 - ((x >> 1) & 1), 0, keepdims=False)
    gradient = gradient.reshape(row_count, col_count, probe_count, levels)
    scaled = spread[:, :, None, :] * gradient
    edges = swap_edges(*edge_rows(scaled, NSTEP))
    trace_share = (
        jnp.sum(shares[:, 0, 0])
        * (1.0 / (probe_count * lev_count * tile_count * slot_count * channels))
    ).reshape(1)
    edges, trace_share = lax.optimization_barrier((edges, trace_share))
    hessian = spread_tile(
        me.reshape(1), scaled.reshape(-1, levels), *(e.reshape(-1, levels) for e in edges), rate
    ).reshape(scaled.shape)
    return (hessian, trace_share)


def solution(mesh):
    placed = (
        P("tile", None, "lev", None),
        P("tile", None, None),
        P(),
        P("tile", None),
        P("tile", None, None),
        P("tile", None, None),
        P(),
        P(),
    )
    return jax.shard_map(
        body,
        mesh=mesh,
        in_specs=placed,
        out_specs=(P("tile", None, "lev", None), P("tile")),
        check_vma=False,
    )
```

```python
import jax
import jax.numpy as jnp
from jax import lax
from jax.experimental import pallas as pl
from jax.experimental.pallas import tpu as pltpu
from jax.sharding import PartitionSpec as P

NSTEP = 2
ZS, XS, CS = 16, 4, 2
QS = XS * CS


def tile_groups(sizes, free):
    groups = {}
    for z in range(sizes[0]):
        for x in range(sizes[1]):
            for c in range(sizes[2]):
                key = tuple(v for i, v in enumerate((z, x, c)) if i not in free)
                groups.setdefault(key, []).append((z * sizes[1] + x) * sizes[2] + c)
    return list(groups.values())


def laplace_step(ext, diffusivity):
    middle = ext[1:-1]
    padded = jnp.pad(middle, ((0, 0), (1, 1), (0, 0), (0, 0)))
    laplace = ext[2:] + ext[:-2] + padded[:, 2:] + padded[:, :-2] - 4.0 * middle
    return middle + diffusivity * laplace


def edge_rows(field, width):
    even = (lax.axis_index("tile") & 1) == 0
    top, bottom = field[:width], field[-width:]
    return jnp.where(even, top, bottom), jnp.where(even, bottom, top)


def cross_pairs(count):
    return [(i, (i - 1 if i % 2 == 0 else i + 1) % count) for i in range(count)]


def swap_edges(to_cross, to_near):
    count = lax.axis_size("tile")
    cross = lax.ppermute(to_cross, "tile", cross_pairs(count))
    near = lax.ppermute(to_near, "tile", [(i, i ^ 1) for i in range(count)])
    return cross, near


def in_vmem(*arrays):
    return [pltpu.with_memory_space_constraint(a, pltpu.VMEM) for a in arrays]


def stage_kernel(
    me_ref, probes, jac, stddev, diffusivity, columns, counts,
    to_cross, to_near, copies, field, spread, rate, out,
):
    edge = to_cross.shape[0]
    even = (me_ref[0] & 1) == 0
    top, bottom = probes[:edge], probes[-edge:]
    to_cross[...] = jnp.where(even, top, bottom)
    to_near[...] = jnp.where(even, bottom, top)
    for z in range(copies.shape[0]):
        copies[z] = jac[...]
    field[...] = probes[...].astype(jnp.float32)
    spread[...] = stddev[...]
    rate[...] = diffusivity[...]
    slots, sections = columns.shape
    width = out.shape[1]
    live = lax.broadcasted_iota(jnp.int32, (slots, sections), 0) < counts[...]
    target = jnp.where(live, columns[...], -1).astype(jnp.float32).astype(jnp.bfloat16)
    lane = lax.broadcasted_iota(jnp.int32, (sections, width), 1)
    apart = lax.broadcasted_iota(jnp.int32, (sections, width), 0) - (lane >> 4) * QS
    slot = lax.broadcasted_iota(jnp.int32, (slots, width), 0)
    mine = slot == (lax.broadcasted_iota(jnp.int32, (slots, width), 1) & (slots - 1))
    lines = []
    for q in range(QS):
        choose = jnp.where(apart == q, 1.0, 0.0).astype(jnp.bfloat16)
        spread = jnp.dot(target, choose, preferred_element_type=jnp.float32)
        lines.append(jnp.sum(jnp.where(mine, spread, 0.0), axis=0, keepdims=True))
    out[...] = jnp.concatenate(lines, axis=0).astype(jnp.bfloat16)


def stage(me, probes, jac, stddev, diffusivity, columns, counts, edge):
    vmem = pl.BlockSpec(memory_space=pltpu.VMEM)
    rows = pltpu.VMEM((edge, probes.shape[1]), probes.dtype)
    return pl.pallas_call(
        stage_kernel,
        out_shape=(
            rows,
            rows,
            jax.ShapeDtypeStruct((ZS,) + jac.shape, jac.dtype),
            pltpu.VMEM(probes.shape, jnp.float32),
            pltpu.VMEM(stddev.shape, jnp.float32),
            pltpu.VMEM(diffusivity.shape, jnp.float32),
            pltpu.VMEM((QS, columns.size // QS), jnp.bfloat16),
        ),
        in_specs=[pl.BlockSpec(memory_space=pltpu.SMEM)] + [vmem] * 6,
        out_specs=(vmem,) * 7,
        name="stage",
    )(me, probes, jac, stddev, diffusivity, columns, counts)


def spread_kernel(me_ref, scaled, cross, near, rate, out):
    wide = cross.shape[0] // NSTEP
    even = (me_ref[0] & 1) == 0
    before = jnp.where(even, cross[...], near[...])
    after = jnp.where(even, near[...], cross[...])
    tile = scaled[...]
    grid = [b[i : i + wide] for b in (before, tile, after) for i in range(0, b.shape[0], wide)]
    place = lax.broadcasted_iota(jnp.int32, (wide, scaled.shape[1]), 0)
    speed = rate[...]
    for _ in range(NSTEP):
        new = []
        for i in range(1, len(grid) - 1):
            middle = grid[i]
            following = jnp.where(place >= wide - 2, 0.0, pltpu.roll(middle, wide - 2, 0))
            leading = jnp.where(place < 2, 0.0, pltpu.roll(middle, 2, 0))
            laplace = grid[i + 1] + grid[i - 1] + following + leading - 4.0 * middle
            new.append(middle + speed * laplace)
        grid = new
    for i, row in enumerate(grid):
        out[i * wide : (i + 1) * wide] = row


def spread_tile(me, scaled, cross, near, rate):
    vmem = pl.BlockSpec(memory_space=pltpu.VMEM)
    return pl.pallas_call(
        spread_kernel,
        out_shape=jax.ShapeDtypeStruct(scaled.shape, jnp.float32),
        in_specs=[pl.BlockSpec(memory_space=pltpu.SMEM)] + [vmem] * 4,
        out_specs=vmem,
        name="diffuse",
    )(me, *in_vmem(scaled, cross, near, rate))


def band_columns(jac, offsets):
    band, ch = jac.shape

    def zeros(n):
        return jnp.zeros((n, ch), jac.dtype)

    x = jnp.concatenate([jac, zeros(8)], axis=0)
    for shift in (1, 2, 4):
        x = jnp.where((offsets & shift) != 0, pltpu.roll(x, shift, 0), x)
    for shift in (8, 16, 32):
        down = jnp.concatenate([zeros(shift), x], axis=0)
        stay = jnp.concatenate([x, zeros(shift)], axis=0)
        x = jnp.where((offsets & shift) != 0, down, stay)
    far = (offsets & 64) != 0
    top = jnp.where(far, zeros(64), x[:64])
    low = jnp.where(far, x[:64], jnp.concatenate([x[64:96], zeros(32)], axis=0))
    return jnp.concatenate([top, low], axis=0)


def respond_kernel(me_ref, gathered, jac, off, wts, mine, other, energy, sel, rows, adj):
    tiles, cells_ext, width = gathered.shape
    cells = sel.shape[1]
    sections = jac.shape[0]
    lev = width // 2
    slot = rows.shape[1] // sections
    me = me_ref[0]
    cell_id = lax.broadcasted_iota(jnp.int32, (cells, rows.shape[1]), 0).astype(jnp.float32)
    pick = lax.broadcasted_iota(jnp.int32, (tiles, width), 0) == me
    for q in range(tiles):
        block = gathered[q, cells : cells + tiles, :].astype(jnp.float32)
        target = jnp.sum(jnp.where(pick, block, 0.0), axis=0, keepdims=True)
        chosen = jnp.where(cell_id == target, 1.0, 0.0).astype(jnp.bfloat16)
        sel[q] = chosen
        rows[q] = lax.dot_general(
            chosen,
            gathered[q, :cells, :],
            (((0,), (0,)), ((), ())),
            preferred_element_type=jnp.float32,
        ).astype(jnp.bfloat16)
    for s in range(sections):
        row = pl.ds(s * tiles + me, 1)
        band = band_columns(jac[s].astype(jnp.float32), off[row, :]).astype(jnp.bfloat16)
        here = slice(s * slot, (s + 1) * slot)
        weight = wts[row, :]
        total = jnp.zeros((1, band.shape[1]), jnp.float32)
        for h in range(2):
            span = range(h * tiles // 2, (h + 1) * tiles // 2)
            mine_rows = jnp.concatenate(
                [rows[q, here, p * lev : (p + 1) * lev] for q in span for p in range(2)], axis=0
            )
            bright = jnp.dot(mine_rows, band, preferred_element_type=jnp.float32)
            weighted = weight * bright
            total = total + jnp.sum(bright * weighted, axis=0, keepdims=True)
            back = lax.dot_general(
                weighted.astype(jnp.bfloat16),
                band,
                (((1,), (1,)), ((), ())),
                preferred_element_type=jnp.float32,
            ).astype(jnp.bfloat16)
            at = 0
            for q in span:
                for p in range(2):
                    adj[q, here, p * lev : (p + 1) * lev] = back[at : at + slot]
                    at += slot
        each = energy.shape[0] // sections
        energy[s * each : (s + 1) * each] = jnp.broadcast_to(
            jnp.sum(total, axis=1, keepdims=True)[None], (each,) + energy.shape[1:]
        )
    for half, out in ((0, mine), (1, other)):
        late = 3 - 2 * ((me ^ half) & 1)
        for j, away in enumerate((0, late, 4 - late, 2)):
            q = me ^ (CS * away + half)
            out[j] = jnp.dot(sel[q], adj[q], preferred_element_type=jnp.float32)


def respond_all(me, gathered, jac, off, wts, copies):
    tiles, cells_ext, width = gathered.shape
    cells = cells_ext - tiles
    sections = jac.shape[0]
    part = pltpu.VMEM((tiles // 2, cells, width), jnp.float32)
    vmem = pl.BlockSpec(memory_space=pltpu.VMEM)
    return pl.pallas_call(
        respond_kernel,
        out_shape=(part, part, pltpu.VMEM((sections * copies, 1, 128), jnp.float32)),
        in_specs=[pl.BlockSpec(memory_space=pltpu.SMEM), vmem, vmem, vmem, vmem],
        out_specs=(vmem, vmem, vmem),
        scratch_shapes=[
            pltpu.VMEM((tiles, cells, 256), jnp.bfloat16),
            pltpu.VMEM((tiles, 256, width), jnp.bfloat16),
            pltpu.VMEM((tiles, 256, width), jnp.bfloat16),
        ],
        name="respond",
    )(me, *in_vmem(gathered, jac, off, wts))


def body(probes, stddev, diffusivity, counts, columns, jacobian, offsets, obs_weights):
    tile_count = lax.axis_size("tile")
    row_count, col_count, probe_count, levels = probes.shape
    slot_count = columns.shape[2]
    channels = jacobian.shape[1]
    cell_count = row_count * col_count
    sizes = (ZS, XS, CS)
    along_z = tile_groups(sizes, (0,))
    along_x = tile_groups(sizes, (1,))
    plane = tile_groups(sizes, (1, 2))
    here = lax.axis_index("tile")
    me = here & (QS - 1)
    to_cross, to_near, copies, field, spread, rate, targets = stage(
        me.reshape(1), probes.reshape(-1, levels), jacobian[0].T, stddev, diffusivity[None],
        columns[0].T, counts, NSTEP * col_count * probe_count,
    )
    jac = lax.all_to_all(copies, "tile", 0, 0, axis_index_groups=along_z, tiled=True)
    rows = (NSTEP, col_count, probe_count, levels)
    cross = lax.ppermute(to_cross, "tile", cross_pairs(tile_count))
    to_near, cross = lax.optimization_barrier((to_near, cross))
    near = lax.all_gather(
        to_near, "tile", axis=0, axis_index_groups=tile_groups(sizes, (2,)),
    )
    near = lax.dynamic_index_in_dim(near, 1 - (me & 1), 0, keepdims=False)
    cross, near = cross.reshape(rows), near.reshape(rows)
    even = (me & 1) == 0
    ext = jnp.concatenate(
        [
            jnp.where(even, cross, near).astype(jnp.float32),
            field.reshape(probes.shape),
            jnp.where(even, near, cross).astype(jnp.float32),
        ],
        axis=0,
    )
    for _ in range(NSTEP):
        ext = laplace_step(ext, rate[0])
    profile = (spread[:, :, None, :] * ext).astype(jnp.bfloat16)
    block = jnp.concatenate([profile.reshape(cell_count, -1), targets], axis=0)
    gathered = lax.all_gather(
        block[None],
        "tile", axis=0, axis_index_groups=plane, tiled=True,
    )
    lev_count = lax.axis_size("lev")
    mine, other, energy = respond_all(me.reshape(1), gathered, jac, offsets, obs_weights, lev_count)
    along_zy = [[t * lev_count + y for t in group for y in range(lev_count)] for group in along_z]
    shares = lax.all_to_all(energy, ("tile", "lev"), 0, 0, axis_index_groups=along_zy, tiled=True)
    summed = mine + lax.ppermute(other, "tile", [(i, i ^ 1) for i in range(tile_count)])
    x = (here >> 1) & (XS - 1)
    even = (here & 1) == 0
    low, high = x & 1, x >> 1
    steps = [
        [[t, t ^ (CS * k[t & 1])] for t in range(tile_count) if t < t ^ (CS * k[t & 1])]
        for k in ((1, 3), (3, 1))
    ]
    sent = lax.all_gather(summed[2:], "tile", axis=0, axis_index_groups=steps[0])
    part = 1 - jnp.where(even, low, high)
    halves = summed[:2] + lax.dynamic_index_in_dim(sent, part, 0, keepdims=False)
    sent = lax.all_gather(halves[1], "tile", axis=0, axis_index_groups=steps[1])
    part = 1 - jnp.where(even, high, low)
    gradient = halves[0] + lax.dynamic_index_in_dim(sent, part, 0, keepdims=False)
    gradient = gradient.reshape(row_count, col_count, probe_count, levels)
    scaled = spread[:, :, None, :] * gradient
    edges = swap_edges(*edge_rows(scaled, NSTEP))
    trace_share = (
        jnp.sum(shares[:, 0, 0])
        * (1.0 / (probe_count * lev_count * tile_count * slot_count * channels))
    ).reshape(1)
    edges, trace_share = lax.optimization_barrier((edges, trace_share))
    hessian = spread_tile(
        me.reshape(1), scaled.reshape(-1, levels), *(e.reshape(-1, levels) for e in edges), rate
    ).reshape(scaled.shape)
    return (hessian, trace_share)


def solution(mesh):
    placed = (
        P("tile", None, "lev", None),
        P("tile", None, None),
        P(),
        P("tile", None),
        P("tile", None, None),
        P("tile", None, None),
        P(),
        P(),
    )
    return jax.shard_map(
        body,
        mesh=mesh,
        in_specs=placed,
        out_specs=(P("tile", None, "lev", None), P("tile")),
        check_vma=False,
    )
```

```python
import jax
import jax.numpy as jnp
from jax import lax
from jax.experimental import pallas as pl
from jax.experimental.pallas import tpu as pltpu
from jax.sharding import PartitionSpec as P

NSTEP = 2
ZS, XS, CS = 16, 4, 2
QS = XS * CS


def tile_groups(sizes, free):
    groups = {}
    for z in range(sizes[0]):
        for x in range(sizes[1]):
            for c in range(sizes[2]):
                key = tuple(v for i, v in enumerate((z, x, c)) if i not in free)
                groups.setdefault(key, []).append((z * sizes[1] + x) * sizes[2] + c)
    return list(groups.values())


def laplace_step(ext, diffusivity):
    middle = ext[1:-1]
    padded = jnp.pad(middle, ((0, 0), (1, 1), (0, 0), (0, 0)))
    laplace = ext[2:] + ext[:-2] + padded[:, 2:] + padded[:, :-2] - 4.0 * middle
    return middle + diffusivity * laplace


def edge_rows(field, width):
    even = (lax.axis_index("tile") & 1) == 0
    top, bottom = field[:width], field[-width:]
    return jnp.where(even, top, bottom), jnp.where(even, bottom, top)


def cross_pairs(count):
    return [(i, (i - 1 if i % 2 == 0 else i + 1) % count) for i in range(count)]


def swap_edges(to_cross, to_near):
    count = lax.axis_size("tile")
    cross = lax.ppermute(to_cross, "tile", cross_pairs(count))
    near = lax.ppermute(to_near, "tile", [(i, i ^ 1) for i in range(count)])
    return cross, near


def in_vmem(*arrays):
    return [pltpu.with_memory_space_constraint(a, pltpu.VMEM) for a in arrays]


def stage_kernel(
    me_ref, probes, jac, stddev, diffusivity, columns, counts,
    to_cross, to_near, copies, field, spread, rate, out,
):
    edge = to_cross.shape[0]
    even = (me_ref[0] & 1) == 0
    top, bottom = probes[:edge], probes[-edge:]
    to_cross[...] = jnp.where(even, top, bottom)
    to_near[...] = jnp.where(even, bottom, top)
    for z in range(copies.shape[0]):
        copies[z] = jac[...]
    field[...] = probes[...].astype(jnp.float32)
    spread[...] = stddev[...]
    rate[...] = diffusivity[...]
    slots, sections = columns.shape
    width = out.shape[1]
    live = lax.broadcasted_iota(jnp.int32, (slots, sections), 0) < counts[...]
    target = jnp.where(live, columns[...], -1).astype(jnp.float32).astype(jnp.bfloat16)
    lane = lax.broadcasted_iota(jnp.int32, (sections, width), 1)
    apart = lax.broadcasted_iota(jnp.int32, (sections, width), 0) - (lane >> 4) * QS
    slot = lax.broadcasted_iota(jnp.int32, (slots, width), 0)
    mine = slot == (lax.broadcasted_iota(jnp.int32, (slots, width), 1) & (slots - 1))
    lines = []
    for q in range(QS):
        choose = jnp.where(apart == q, 1.0, 0.0).astype(jnp.bfloat16)
        spread = jnp.dot(target, choose, preferred_element_type=jnp.float32)
        lines.append(jnp.sum(jnp.where(mine, spread, 0.0), axis=0, keepdims=True))
    out[...] = jnp.concatenate(lines, axis=0).astype(jnp.bfloat16)


def stage(me, probes, jac, stddev, diffusivity, columns, counts, edge):
    vmem = pl.BlockSpec(memory_space=pltpu.VMEM)
    rows = pltpu.VMEM((edge, probes.shape[1]), probes.dtype)
    return pl.pallas_call(
        stage_kernel,
        out_shape=(
            rows,
            rows,
            pltpu.VMEM((ZS,) + jac.shape, jac.dtype),
            pltpu.VMEM(probes.shape, jnp.float32),
            pltpu.VMEM(stddev.shape, jnp.float32),
            pltpu.VMEM(diffusivity.shape, jnp.float32),
            pltpu.VMEM((QS, columns.size // QS), jnp.bfloat16),
        ),
        in_specs=[pl.BlockSpec(memory_space=pltpu.SMEM)] + [vmem] * 6,
        out_specs=(vmem,) * 7,
        name="stage",
    )(me, probes, jac, stddev, diffusivity, columns, counts)


def spread_kernel(me_ref, scaled, cross, near, rate, out):
    wide = cross.shape[0] // NSTEP
    even = (me_ref[0] & 1) == 0
    before = jnp.where(even, cross[...], near[...])
    after = jnp.where(even, near[...], cross[...])
    tile = scaled[...]
    grid = [b[i : i + wide] for b in (before, tile, after) for i in range(0, b.shape[0], wide)]
    place = lax.broadcasted_iota(jnp.int32, (wide, scaled.shape[1]), 0)
    speed = rate[...]
    for _ in range(NSTEP):
        new = []
        for i in range(1, len(grid) - 1):
            middle = grid[i]
            following = jnp.where(place >= wide - 2, 0.0, pltpu.roll(middle, wide - 2, 0))
            leading = jnp.where(place < 2, 0.0, pltpu.roll(middle, 2, 0))
            laplace = grid[i + 1] + grid[i - 1] + following + leading - 4.0 * middle
            new.append(middle + speed * laplace)
        grid = new
    for i, row in enumerate(grid):
        out[i * wide : (i + 1) * wide] = row


def spread_tile(me, scaled, cross, near, rate):
    vmem = pl.BlockSpec(memory_space=pltpu.VMEM)
    return pl.pallas_call(
        spread_kernel,
        out_shape=jax.ShapeDtypeStruct(scaled.shape, jnp.float32),
        in_specs=[pl.BlockSpec(memory_space=pltpu.SMEM)] + [vmem] * 4,
        out_specs=vmem,
        name="diffuse",
    )(me, *in_vmem(scaled, cross, near, rate))


def band_columns(jac, offsets):
    band, ch = jac.shape

    def zeros(n):
        return jnp.zeros((n, ch), jac.dtype)

    x = jnp.concatenate([jac, zeros(8)], axis=0)
    for shift in (1, 2, 4):
        x = jnp.where((offsets & shift) != 0, pltpu.roll(x, shift, 0), x)
    for shift in (8, 16, 32):
        down = jnp.concatenate([zeros(shift), x], axis=0)
        stay = jnp.concatenate([x, zeros(shift)], axis=0)
        x = jnp.where((offsets & shift) != 0, down, stay)
    far = (offsets & 64) != 0
    top = jnp.where(far, zeros(64), x[:64])
    low = jnp.where(far, x[:64], jnp.concatenate([x[64:96], zeros(32)], axis=0))
    return jnp.concatenate([top, low], axis=0)


def respond_kernel(me_ref, gathered, jac, off, wts, mine, other, energy, sel, rows, adj):
    tiles, cells_ext, width = gathered.shape
    cells = sel.shape[1]
    sections = jac.shape[0]
    lev = width // 2
    slot = rows.shape[1] // sections
    me = me_ref[0]
    cell_id = lax.broadcasted_iota(jnp.int32, (cells, rows.shape[1]), 0).astype(jnp.float32)
    pick = lax.broadcasted_iota(jnp.int32, (tiles, width), 0) == me
    for q in range(tiles):
        block = gathered[q, cells : cells + tiles, :].astype(jnp.float32)
        target = jnp.sum(jnp.where(pick, block, 0.0), axis=0, keepdims=True)
        chosen = jnp.where(cell_id == target, 1.0, 0.0).astype(jnp.bfloat16)
        sel[q] = chosen
        rows[q] = lax.dot_general(
            chosen,
            gathered[q, :cells, :],
            (((0,), (0,)), ((), ())),
            preferred_element_type=jnp.float32,
        ).astype(jnp.bfloat16)
    for s in range(sections):
        row = pl.ds(s * tiles + me, 1)
        band = band_columns(jac[s].astype(jnp.float32), off[row, :]).astype(jnp.bfloat16)
        here = slice(s * slot, (s + 1) * slot)
        weight = wts[row, :]
        total = jnp.zeros((1, band.shape[1]), jnp.float32)
        for h in range(2):
            span = range(h * tiles // 2, (h + 1) * tiles // 2)
            mine_rows = jnp.concatenate(
                [rows[q, here, p * lev : (p + 1) * lev] for q in span for p in range(2)], axis=0
            )
            bright = jnp.dot(mine_rows, band, preferred_element_type=jnp.float32)
            weighted = weight * bright
            total = total + jnp.sum(bright * weighted, axis=0, keepdims=True)
            back = lax.dot_general(
                weighted.astype(jnp.bfloat16),
                band,
                (((1,), (1,)), ((), ())),
                preferred_element_type=jnp.float32,
            ).astype(jnp.bfloat16)
            at = 0
            for q in span:
                for p in range(2):
                    adj[q, here, p * lev : (p + 1) * lev] = back[at : at + slot]
                    at += slot
        each = energy.shape[0] // sections
        energy[s * each : (s + 1) * each] = jnp.broadcast_to(
            jnp.sum(total, axis=1, keepdims=True)[None], (each,) + energy.shape[1:]
        )
    for half, out in ((0, mine), (1, other)):
        late = 3 - 2 * ((me ^ half) & 1)
        for j, away in enumerate((0, late, 4 - late, 2)):
            q = me ^ (CS * away + half)
            out[j] = jnp.dot(sel[q], adj[q], preferred_element_type=jnp.float32)


def respond_all(me, gathered, jac, off, wts, copies):
    tiles, cells_ext, width = gathered.shape
    cells = cells_ext - tiles
    sections = jac.shape[0]
    part = pltpu.VMEM((tiles // 2, cells, width), jnp.float32)
    vmem = pl.BlockSpec(memory_space=pltpu.VMEM)
    return pl.pallas_call(
        respond_kernel,
        out_shape=(part, part, pltpu.VMEM((sections * copies, 1, 128), jnp.float32)),
        in_specs=[pl.BlockSpec(memory_space=pltpu.SMEM), vmem, vmem, vmem, vmem],
        out_specs=(vmem, vmem, vmem),
        scratch_shapes=[
            pltpu.VMEM((tiles, cells, 256), jnp.bfloat16),
            pltpu.VMEM((tiles, 256, width), jnp.bfloat16),
            pltpu.VMEM((tiles, 256, width), jnp.bfloat16),
        ],
        name="respond",
    )(me, *in_vmem(gathered, jac, off, wts))


def body(probes, stddev, diffusivity, counts, columns, jacobian, offsets, obs_weights):
    tile_count = lax.axis_size("tile")
    row_count, col_count, probe_count, levels = probes.shape
    slot_count = columns.shape[2]
    channels = jacobian.shape[1]
    cell_count = row_count * col_count
    sizes = (ZS, XS, CS)
    along_z = tile_groups(sizes, (0,))
    along_x = tile_groups(sizes, (1,))
    plane = tile_groups(sizes, (1, 2))
    here = lax.axis_index("tile")
    me = here & (QS - 1)
    to_cross, to_near, copies, field, spread, rate, targets = stage(
        me.reshape(1), probes.reshape(-1, levels), jacobian[0].T, stddev, diffusivity[None],
        columns[0].T, counts, NSTEP * col_count * probe_count,
    )
    jac = lax.all_to_all(copies, "tile", 0, 0, axis_index_groups=along_z, tiled=True)
    rows = (NSTEP, col_count, probe_count, levels)
    cross = lax.ppermute(to_cross, "tile", cross_pairs(tile_count))
    to_near, cross = lax.optimization_barrier((to_near, cross))
    near = lax.all_gather(
        to_near, "tile", axis=0, axis_index_groups=tile_groups(sizes, (2,)),
    )
    near = lax.dynamic_index_in_dim(near, 1 - (me & 1), 0, keepdims=False)
    cross, near = cross.reshape(rows), near.reshape(rows)
    even = (me & 1) == 0
    ext = jnp.concatenate(
        [
            jnp.where(even, cross, near).astype(jnp.float32),
            field.reshape(probes.shape),
            jnp.where(even, near, cross).astype(jnp.float32),
        ],
        axis=0,
    )
    for _ in range(NSTEP):
        ext = laplace_step(ext, rate[0])
    profile = (spread[:, :, None, :] * ext).astype(jnp.bfloat16)
    block = jnp.concatenate([profile.reshape(cell_count, -1), targets], axis=0)
    gathered = lax.all_gather(
        block[None],
        "tile", axis=0, axis_index_groups=plane, tiled=True,
    )
    lev_count = lax.axis_size("lev")
    mine, other, energy = respond_all(me.reshape(1), gathered, jac, offsets, obs_weights, lev_count)
    along_zy = [[t * lev_count + y for t in group for y in range(lev_count)] for group in along_z]
    shares = lax.all_to_all(energy, ("tile", "lev"), 0, 0, axis_index_groups=along_zy, tiled=True)
    summed = mine + lax.ppermute(other, "tile", [(i, i ^ 1) for i in range(tile_count)])
    x = (here >> 1) & (XS - 1)
    even = (here & 1) == 0
    low, high = x & 1, x >> 1
    steps = [
        [[t, t ^ (CS * k[t & 1])] for t in range(tile_count) if t < t ^ (CS * k[t & 1])]
        for k in ((1, 3), (3, 1))
    ]
    sent = lax.all_gather(summed[2:], "tile", axis=0, axis_index_groups=steps[0])
    part = 1 - jnp.where(even, low, high)
    halves = summed[:2] + lax.dynamic_index_in_dim(sent, part, 0, keepdims=False)
    sent = lax.all_gather(halves[1], "tile", axis=0, axis_index_groups=steps[1])
    part = 1 - jnp.where(even, high, low)
    gradient = halves[0] + lax.dynamic_index_in_dim(sent, part, 0, keepdims=False)
    gradient = gradient.reshape(row_count, col_count, probe_count, levels)
    scaled = spread[:, :, None, :] * gradient
    edges = swap_edges(*edge_rows(scaled, NSTEP))
    trace_share = (
        jnp.sum(shares[:, 0, 0])
        * (1.0 / (probe_count * lev_count * tile_count * slot_count * channels))
    ).reshape(1)
    edges, trace_share = lax.optimization_barrier((edges, trace_share))
    hessian = spread_tile(
        me.reshape(1), scaled.reshape(-1, levels), *(e.reshape(-1, levels) for e in edges), rate
    ).reshape(scaled.shape)
    return (hessian, trace_share)


def solution(mesh):
    placed = (
        P("tile", None, "lev", None),
        P("tile", None, None),
        P(),
        P("tile", None),
        P("tile", None, None),
        P("tile", None, None),
        P(),
        P(),
    )
    return jax.shard_map(
        body,
        mesh=mesh,
        in_specs=placed,
        out_specs=(P("tile", None, "lev", None), P("tile")),
        check_vma=False,
    )
```
